32 devices in a mesh: lag: 4 (over z), elem: 8 (over y, x, core).
Axes of the slice: x: 2, y: 2, z: 4, core: 2. Of those that a mesh axis runs over, the one named last changes fastest.
Arguments:
- kernel_tiles: bfloat16 [4, 8192, 1536], P('lag', 'elem'), may hold values from -0.078125 to 0.078125
- shell_index: int32 [4, 8, 3], P('lag', 'elem'), may hold values from 0 to 5
- cone_blocks: int32 [4], P('lag'), may hold values from 1 to 3
- history: bfloat16 [4, 8192, 256], P('lag', 'elem'), may hold values from -6 to 6
- prestress: float32 [8, 4, 256, 256], P('elem', 'lag'), may hold values from -6 to 6
- log_state: float32 [8, 4, 256, 256], P('elem', 'lag'), may hold values from -0.7 to 0.7
- fric_a: float32 [8, 4, 256], P('elem', 'lag'), may hold values from 0.3 to 1
- fric_b: float32 [8, 4, 256], P('elem', 'lag'), may hold values from 0.3 to 1
- normal_stress: float32 [8, 4, 256], P('elem', 'lag'), may hold values from 1 to 4
Outputs:
- final_rates: bfloat16 [8, 4, 256, 256], P('elem', 'lag')
- final_state: float32 [8, 4, 256, 256], P('elem', 'lag')
The draws below stay inside these ranges and needn't reach their ends.
Inputs may be any that keep to these rules, and one draw needn't show every extreme that they name: `shell_index`: 0 and 1 name the two blocks of the element block below the receiver block, 2 and 3 its own, 4 and 5 those of the block above.
All inputs are finite; a program needn't handle non-finite values.
Results may differ from the reference program's by a relative error of at most 0.0034.
Values may be sent and summed in bfloat16 or wider, within the bound.
No kernel may reach another device: no remote copies, remote signals or barrier semaphores. Data moves between devices by JAX's collectives and lax.ppermute only.
A program may use at most 64 MiB of HBM per device.

```python
import math
import jax
import jax.numpy as jnp
from jax import lax

ELEM_DEV = 1024
BLOCK = 512
SHELL = 3
SCENARIOS = 256
STEPS = 4
NEWTON = 3
LAGS = 4
ELEMS = 8192
ROWS = 256
N_LAG = 4
N_ELEM = 8


def set_ends(entries, rng, smallest, high):
    longest = entries.shape.index(max(entries.shape))
    spots = []
    for shift in (0, 1):
        where = [jax.random.randint(jax.random.fold_in(rng, axis), (), 0, length) for axis, length in enumerate(entries.shape)]
        where[longest] = (where[longest] + shift) % entries.shape[longest]
        spots.append(tuple(where))
    return entries.at[spots[0]].set(smallest).at[spots[1]].set(high)


def steps_of(rng, extent, shards, least, top_value):
    gain, own = 1.0, jax.random.fold_in(rng, 6)
    for position, blocks in shards:
        heights = jnp.exp(jax.random.uniform(jax.random.fold_in(own, position), (blocks,), jnp.float32, least / len(shards), top_value / len(shards)))
        gain = gain * jnp.repeat(heights, extent[position] // blocks).reshape([-1 if axis == position else 1 for axis in range(len(extent))])
    return gain


def normal_values(own_key, extent, spread, most, pieces=(), kind=jnp.bfloat16):
    result = spread * jax.random.normal(own_key, extent, jnp.float32)
    if pieces:
        result = result * steps_of(own_key, extent, pieces, -0.22, 0.18)
    return jnp.clip(result, -most, most).astype(kind)


def setup_inputs(seed: int = 0) -> dict:
    seeds = jax.random.split(jax.random.key(seed), 10)
    return {
        "kernel_tiles": normal_values(seeds[0], (LAGS, ELEMS, SHELL * BLOCK), (SHELL * BLOCK * N_LAG) ** -0.5, 0.078125, ((0, 4), (1, 8))),
        "shell_index": set_ends(jax.random.randint(seeds[1], (LAGS, N_ELEM, SHELL), 0, 6), jax.random.fold_in(seeds[1], 1), 0, 5).astype(jnp.int32),
        "cone_blocks": set_ends(jax.random.randint(seeds[2], (LAGS,), 1, SHELL + 1), jax.random.fold_in(seeds[2], 1), 1, SHELL).astype(jnp.int32),
        "history": normal_values(seeds[3], (LAGS, ELEMS, SCENARIOS), 1.0, 6.0, ((0, 4), (1, 8))),
        "prestress": normal_values(seeds[4], (N_ELEM, N_LAG, ROWS, SCENARIOS), 1.0, 6.0, ((0, 8), (1, 4)), jnp.float32),
        "log_state": jnp.clip(jax.random.uniform(seeds[5], (N_ELEM, N_LAG, ROWS, SCENARIOS), jnp.float32, -0.7, 0.7) * steps_of(seeds[5], (N_ELEM, N_LAG, ROWS, SCENARIOS), ((0, 8), (1, 4)), -0.4, 0.0), -0.7, 0.7),
        "fric_a": jnp.clip(jnp.exp(math.log(1.0) - 1.2039728 * jax.random.uniform(seeds[6], (N_ELEM, N_LAG, ROWS), jnp.float32) ** steps_of(seeds[6], (N_ELEM, N_LAG, ROWS), ((0, 8), (1, 4)), -0.2, 0.2)), 0.3, 1.0),
        "fric_b": jnp.clip(jnp.exp(math.log(1.0) - 1.2039728 * jax.random.uniform(seeds[7], (N_ELEM, N_LAG, ROWS), jnp.float32) ** steps_of(seeds[7], (N_ELEM, N_LAG, ROWS), ((0, 8), (1, 4)), -0.2, 0.2)), 0.3, 1.0),
        "normal_stress": jnp.clip(jnp.exp(math.log(4.0) - 1.3862944 * jax.random.uniform(seeds[8], (N_ELEM, N_LAG, ROWS), jnp.float32) ** steps_of(seeds[8], (N_ELEM, N_LAG, ROWS), ((0, 8), (1, 4)), -0.2, 0.2)), 1.0, 4.0),
    }


damping = 0.5
time_step = 0.25
creep_square = 0.01

def inverse_sinh(value):
    magnitude = jnp.abs(value)
    positive = jnp.log(magnitude + jnp.sqrt(magnitude * magnitude + 1.0))
    return jnp.where(value < 0.0, -positive, positive)

def gather_sources(lag_rates, shell_pick, live_count):
    padded = jnp.pad(lag_rates, ((ELEM_DEV, ELEM_DEV), (0, 0)))
    window_start = jnp.arange(N_ELEM, dtype=jnp.int32)[:, None] * ELEM_DEV + shell_pick.astype(jnp.int32) * BLOCK
    row_ids = window_start[:, :, None] + jnp.arange(BLOCK, dtype=jnp.int32)[None, None, :]
    sources = padded[row_ids]
    live_mask = jnp.arange(SHELL, dtype=jnp.int32)[None, :, None, None] < live_count
    sources = jnp.where(live_mask, sources, jnp.zeros((), sources.dtype))
    return sources.reshape(N_ELEM, SHELL * BLOCK, SCENARIOS)

def traction_sum(kernel_tiles, shell_index, cone_blocks, history):

    def one_lag(summed, items):
        kernel_tile, shell_pick, live_count, lag_rates = items
        sources = gather_sources(lag_rates, shell_pick, live_count)
        kernel_rows = kernel_tile.reshape(N_ELEM, ELEM_DEV, SHELL * BLOCK).astype(jnp.float32)
        partial_value = jnp.einsum('erc,ecs->ers', kernel_rows, sources.astype(jnp.float32))
        return (summed + partial_value.reshape(ELEMS, SCENARIOS), None)
    start_sum = jnp.zeros((ELEMS, SCENARIOS), jnp.float32)
    summed, unused = lax.scan(one_lag, start_sum, (kernel_tiles, shell_index, cone_blocks, history))
    return summed

def settle_friction(shear_load, state_now, coef_a, coef_b, sigma):
    scale = 0.5 * jnp.exp(coef_b / coef_a * state_now)
    strength = sigma * coef_a
    velocity = shear_load / (strength * scale + damping)
    for iteration in range(NEWTON):
        scaled = scale * velocity
        residual = strength * inverse_sinh(scaled) + damping * velocity - shear_load
        derivative = strength * scale / jnp.sqrt(1.0 + scaled * scaled) + damping
        velocity = velocity - residual / derivative
    speed = jnp.sqrt(velocity * velocity + creep_square)
    new_state = state_now + time_step * (jnp.exp(-state_now) - speed)
    return (velocity.astype(jnp.bfloat16), new_state)

def reference(kernel_tiles, shell_index, cone_blocks, history, prestress, log_state, fric_a, fric_b, normal_stress):
    stress_flat = prestress.reshape(ELEMS, SCENARIOS)
    state_flat = log_state.reshape(ELEMS, SCENARIOS)
    coef_a = fric_a.reshape(ELEMS, 1)
    coef_b = fric_b.reshape(ELEMS, 1)
    sigma = normal_stress.reshape(ELEMS, 1)
    lag_history = history
    slip_rate = history[0]
    for step_index in range(STEPS):
        traction = traction_sum(kernel_tiles, shell_index, cone_blocks, lag_history)
        slip_rate, state_flat = settle_friction(stress_flat + traction, state_flat, coef_a, coef_b, sigma)
        lag_history = jnp.concatenate([slip_rate[None], lag_history[:-1]], axis=0)
    final_rates = slip_rate.reshape(N_ELEM, N_LAG, ROWS, SCENARIOS)
    final_state = state_flat.reshape(N_ELEM, N_LAG, ROWS, SCENARIOS)
    return (final_rates, final_state)
```

```python
import functools

import jax
import jax.numpy as jnp
from jax import lax
from jax.experimental import pallas as pl
from jax.experimental.pallas import tpu as pltpu
from jax.sharding import PartitionSpec as P

STEPS = 4
NEWTON = 3

damping = 0.5
time_step = 0.25
creep_square = 0.01


def exchange(value):
    count = lax.axis_size("elem")
    up = [(i, i + 1) for i in range(count - 1)]
    down = [(j, i) for i, j in up]
    return lax.ppermute(value, "elem", up), lax.ppermute(value, "elem", down)


def product_kernel(lags, rows, meta, tile, below, own, above, *refs):
    outs, sources, sems = refs[:lags], refs[lags], refs[lags + 1]
    slots = sems.shape[0]
    block = sources.shape[0] // slots
    per = own.shape[0] // block
    live, me = meta[slots], meta[slots + 1]

    for k in range(slots):
        spot = sources.at[pl.ds(k * block, block)]
        pick = meta[k]
        start = pl.multiple_of(lax.rem(pick, per) * block, block)
        for which, ref in enumerate((below, own, above)):

            @pl.when((k < live) & (lax.div(pick, per) == which))
            def _():
                pltpu.make_async_copy(ref.at[pl.ds(start, block)], spot, sems.at[k]).start()

        @pl.when(k >= live)
        def _():
            spot[...] = jnp.zeros(spot.shape, spot.dtype)

    for k in range(slots):
        spot = sources.at[pl.ds(k * block, block)]

        @pl.when(k < live)
        def _():
            pltpu.make_async_copy(own.at[pl.ds(0, block)], spot, sems.at[k]).wait()

    for d in range(lags):
        first = pl.multiple_of(lax.rem(me + d, lags) * rows, rows)
        part = jnp.dot(tile[pl.ds(first, rows), :], sources[...], preferred_element_type=jnp.float32)
        outs[d][...] = part.astype(outs[d].dtype)


def product(meta, tile, below, own, above, lags):
    rows, cols = own.shape[0] // lags, own.shape[1]
    slots = meta.shape[0] - 2
    kernel = functools.partial(product_kernel, lags, rows)
    kinds = [jnp.float32] + [jnp.bfloat16] * (lags - 1)
    return pl.pallas_call(
        kernel,
        grid_spec=pltpu.PrefetchScalarGridSpec(
            num_scalar_prefetch=1,
            grid=(1,),
            in_specs=[pl.BlockSpec(memory_space=pltpu.VMEM)] + [pl.BlockSpec(memory_space=pl.ANY)] * 3,
            out_specs=[pl.BlockSpec(memory_space=pltpu.VMEM)] * lags,
            scratch_shapes=[
                pltpu.VMEM((tile.shape[1], cols), jnp.bfloat16),
                pltpu.SemaphoreType.DMA((slots,)),
            ],
        ),
        out_shape=[jax.ShapeDtypeStruct((rows, cols), kind) for kind in kinds],
        compiler_params=pltpu.CompilerParams(vmem_limit_bytes=24 * 1024 * 1024),
        cost_estimate=pl.CostEstimate(
            flops=2 * tile.size * cols, bytes_accessed=2 * (tile.size + 4 * own.size), transcendentals=0
        ),
        name="product",
    )(meta, tile, below, own, above)


def scatter_sum(parts):
    lags = len(parts)
    total = parts[0]
    for d in range(1, lags):
        route = [(i, (i + d) % lags) for i in range(lags)]
        total = total + lax.ppermute(parts[d], "lag", route).astype(jnp.float32)
    return total


def settle_friction(shear_load, state_now, coef_a, coef_b, sigma):
    scale = 0.5 * jnp.exp(coef_b / coef_a * state_now)
    strength = sigma * coef_a
    velocity = shear_load / (strength * scale + damping)
    for _ in range(NEWTON):
        scaled = scale * velocity
        magnitude = jnp.abs(scaled)
        root = jnp.sqrt(magnitude * magnitude + 1.0)
        positive = jnp.log(magnitude + root)
        arc = jnp.where(scaled < 0.0, -positive, positive)
        residual = strength * arc + damping * velocity - shear_load
        derivative = strength * scale / root + damping
        velocity = velocity - residual / derivative
    speed = jnp.sqrt(velocity * velocity + creep_square)
    new_state = state_now + time_step * (jnp.exp(-state_now) - speed)
    return velocity.astype(jnp.bfloat16), new_state


def shards(kernel_tiles, shell_index, cone_blocks, history, prestress, log_state, fric_a, fric_b, normal_stress):
    lags = lax.axis_size("lag")
    me = lax.axis_index("lag")
    tile, field = kernel_tiles[0], history[0]
    meta = jnp.concatenate([shell_index[0, 0], cone_blocks, me[None].astype(jnp.int32)])
    stress, state = prestress[0, 0], log_state[0, 0]
    coef_a, coef_b = fric_a[0, 0][:, None], fric_b[0, 0][:, None]
    sigma = normal_stress[0, 0][:, None]
    for step in range(STEPS):
        below, above = exchange(field)
        traction = scatter_sum(product(meta, tile, below, field, above, lags))
        rates, state = settle_friction(stress + traction, state, coef_a, coef_b, sigma)
        if step + 1 < STEPS:
            older = lax.ppermute(field, "lag", [(i, i + 1) for i in range(lags - 1)])
            newest = lax.all_gather(rates, "lag", axis=0, tiled=True)
            field = jnp.where(me == 0, newest, older)
    return rates[None, None], state[None, None]


def solution(mesh):
    in_specs = (
        P("lag", "elem", None),
        P("lag", "elem", None),
        P("lag"),
        P("lag", "elem", None),
        P("elem", "lag", None, None),
        P("elem", "lag", None, None),
        P("elem", "lag", None),
        P("elem", "lag", None),
        P("elem", "lag", None),
    )
    out_specs = (P("elem", "lag", None, None), P("elem", "lag", None, None))
    return jax.shard_map(shards, mesh=mesh, in_specs=in_specs, out_specs=out_specs, check_vma=False)
```

```python
import functools

import jax
import jax.numpy as jnp
from jax import lax
from jax.experimental import pallas as pl
from jax.experimental.pallas import tpu as pltpu
from jax.sharding import PartitionSpec as P

STEPS = 4
NEWTON = 3

damping = 0.5
time_step = 0.25
creep_square = 0.01


def exchange(value, planes):
    count = lax.axis_size("elem")
    up = [(i * count + j, i * count + j + 1) for i in planes for j in range(count - 1)]
    down = [(j, i) for i, j in up]
    axes = ("lag", "elem")
    return lax.ppermute(value, axes, up), lax.ppermute(value, axes, down)


def fetch(meta, below, own, above, sources, sems):
    slots = sems.shape[0]
    block = sources.shape[0] // slots
    per = own.shape[0] // block
    live = meta[slots]

    for k in range(slots):
        spot = sources.at[pl.ds(k * block, block)]
        pick = meta[k]
        start = pl.multiple_of(lax.rem(pick, per) * block, block)
        for which, ref in enumerate((below, own, above)):

            @pl.when((k < live) & (lax.div(pick, per) == which))
            def _():
                pltpu.make_async_copy(ref.at[pl.ds(start, block)], spot, sems.at[k]).start()

        @pl.when(k >= live)
        def _():
            spot[...] = jnp.zeros(spot.shape, spot.dtype)

    for k in range(slots):
        spot = sources.at[pl.ds(k * block, block)]

        @pl.when(k < live)
        def _():
            pltpu.make_async_copy(own.at[pl.ds(0, block)], spot, sems.at[k]).wait()


def product_kernel(lags, rows, meta, tile, below, own, above, *refs):
    outs, sources, sems = refs[:lags], refs[lags], refs[lags + 1]
    me = meta[sems.shape[0] + 1]
    fetch(meta, below, own, above, sources, sems)
    for d in range(lags):
        first = pl.multiple_of(lax.rem(me + d, lags) * rows, rows)
        part = jnp.dot(tile[pl.ds(first, rows), :], sources[...], preferred_element_type=jnp.float32)
        outs[d][...] = part.astype(outs[d].dtype)


def product(meta, tile, below, own, above, lags):
    rows, cols = own.shape[0] // lags, own.shape[1]
    slots = meta.shape[0] - 2
    kernel = functools.partial(product_kernel, lags, rows)
    kinds = [jnp.float32] + [jnp.bfloat16] * (lags - 1)
    return pl.pallas_call(
        kernel,
        grid_spec=pltpu.PrefetchScalarGridSpec(
            num_scalar_prefetch=1,
            grid=(1,),
            in_specs=[pl.BlockSpec(memory_space=pltpu.VMEM)] + [pl.BlockSpec(memory_space=pl.ANY)] * 3,
            out_specs=[pl.BlockSpec(memory_space=pltpu.VMEM)] * lags,
            scratch_shapes=[
                pltpu.VMEM((tile.shape[1], cols), jnp.bfloat16),
                pltpu.SemaphoreType.DMA((slots,)),
            ],
        ),
        out_shape=[jax.ShapeDtypeStruct((rows, cols), kind) for kind in kinds],
        compiler_params=pltpu.CompilerParams(vmem_limit_bytes=24 * 1024 * 1024),
        cost_estimate=pl.CostEstimate(
            flops=2 * tile.size * cols, bytes_accessed=2 * (tile.size + 4 * own.size), transcendentals=0
        ),
        name="product",
    )(meta, tile, below, own, above)


def scatter_sum(parts):
    lags = len(parts)
    total = parts[0]
    for d in range(1, lags):
        route = [(i, (i + d) % lags) for i in range(lags)]
        total = total + lax.ppermute(parts[d], "lag", route).astype(jnp.float32)
    return total


def settle_friction(shear_load, state_now, coef_a, coef_b, sigma):
    scale = 0.5 * jnp.exp(coef_b / coef_a * state_now)
    strength = sigma * coef_a
    velocity = shear_load / (strength * scale + damping)
    for _ in range(NEWTON):
        scaled = scale * velocity
        magnitude = jnp.abs(scaled)
        root = jnp.sqrt(magnitude * magnitude + 1.0)
        positive = jnp.log(magnitude + root)
        arc = jnp.where(scaled < 0.0, -positive, positive)
        residual = strength * arc + damping * velocity - shear_load
        derivative = strength * scale / root + damping
        velocity = velocity - residual / derivative
    speed = jnp.sqrt(velocity * velocity + creep_square)
    new_state = state_now + time_step * (jnp.exp(-state_now) - speed)
    return velocity.astype(jnp.bfloat16), new_state


def full_product_kernel(meta, tile, below, own, above, out, sources, sems):
    slots = sems.shape[0]
    active = meta[slots + 1] > 0

    @pl.when(active)
    def _():
        fetch(meta, below, own, above, sources, sems)
        rows = out.shape[0] // 4
        for d in range(4):
            spot = pl.ds(d * rows, rows)
            out[spot, :] = jnp.dot(tile[spot, :], sources[...], preferred_element_type=jnp.float32)

    @pl.when(jnp.logical_not(active))
    def _():
        out[...] = jnp.zeros(out.shape, out.dtype)


def full_product(meta, active, tile, below, own, above):
    slots = meta.shape[0] - 2
    meta = jnp.concatenate([meta[: slots + 1], active.astype(jnp.int32)[None]])
    return pl.pallas_call(
        full_product_kernel,
        grid_spec=pltpu.PrefetchScalarGridSpec(
            num_scalar_prefetch=1,
            grid=(1,),
            in_specs=[pl.BlockSpec(memory_space=pltpu.VMEM)] + [pl.BlockSpec(memory_space=pl.ANY)] * 3,
            out_specs=pl.BlockSpec(memory_space=pltpu.VMEM),
            scratch_shapes=[
                pltpu.VMEM((tile.shape[1], own.shape[1]), jnp.bfloat16),
                pltpu.SemaphoreType.DMA((slots,)),
            ],
        ),
        out_shape=jax.ShapeDtypeStruct(own.shape, jnp.float32),
        compiler_params=pltpu.CompilerParams(vmem_limit_bytes=24 * 1024 * 1024),
        cost_estimate=pl.CostEstimate(
            flops=2 * tile.size * own.shape[1], bytes_accessed=2 * (tile.size + 5 * own.size), transcendentals=0
        ),
        name="full_product",
    )(meta, tile, below, own, above)


def tree_to_first(value, lags, least):
    stride = 1
    while stride < lags:
        route = [(i + stride, i) for i in range(0, lags - stride, 2 * stride) if i + stride >= least]
        value = value + lax.ppermute(value.astype(jnp.bfloat16), "lag", route).astype(jnp.float32)
        stride *= 2
    return value


def shards(kernel_tiles, shell_index, cone_blocks, history, prestress, log_state, fric_a, fric_b, normal_stress):
    lags = lax.axis_size("lag")
    me = lax.axis_index("lag")
    every = range(lags)
    tile, field = kernel_tiles[0], history[0]
    rows = prestress.shape[2]
    meta = jnp.concatenate([shell_index[0, 0], cone_blocks, me[None].astype(jnp.int32)])
    stress, state = prestress[0, 0], log_state[0, 0]
    coefs = [fric_a[0, 0], fric_b[0, 0], normal_stress[0, 0]]
    columns = [c[:, None] for c in coefs]

    below, above = exchange(field, every)
    shifted = lax.ppermute(field, "lag", [(i, i + 1) for i in range(lags - 1)])
    packed = jnp.concatenate([state, jnp.pad(jnp.stack(coefs), ((0, 5), (0, state.shape[1] - rows)))], 0)
    gathered = [packed] + [lax.ppermute(packed, "lag", [(d, 0)]) for d in range(1, lags)]
    parts = product(meta, tile, below, field, above, lags)
    traction = scatter_sum(parts)
    rates, state = settle_friction(stress + traction, state, *columns)

    placed = lax.dynamic_update_slice_in_dim(jnp.zeros(field.shape, jnp.float32), stress, me * rows, 0)
    later = [i for i in every if i >= 1]
    below_1, above_1 = exchange(shifted, later)
    base_1 = tree_to_first(full_product(meta, me >= 1, tile, below_1, shifted, above_1) + placed, lags, 1)
    twice = lax.ppermute(shifted, "lag", [(i, i + 1) for i in range(1, lags - 1)])
    below_2, above_2 = exchange(twice, [i for i in every if i >= 2])
    base_2 = tree_to_first(full_product(meta, me >= 2, tile, below_2, twice, above_2) + placed, lags, 2)

    block_state = jnp.concatenate([g[:rows] for g in gathered], 0)
    block_columns = [jnp.concatenate([g[rows + k, :rows] for g in gathered])[:, None] for k in range(3)]
    first = lax.all_gather(rates, "lag", axis=0, tiled=True)
    speed = jnp.sqrt(jnp.square(first.astype(jnp.float32)) + creep_square)
    block_state = block_state + time_step * (jnp.exp(-block_state) - speed)
    before = block_state

    below_v, above_v = exchange(first, [0, 1])
    part = full_product(meta, me <= 1, tile, below_v, first, above_v)
    from_next = lax.ppermute((part + placed).astype(jnp.bfloat16), "lag", [(1, 0)])
    second, block_state = settle_friction(base_1 + part, block_state, *block_columns)
    below_v, above_v = exchange(second, [0])
    part = full_product(meta, me == 0, tile, below_v, second, above_v)
    sent = jnp.where(me == 0, second, twice)
    moved = lax.ppermute(sent, "lag", [(0, 1)] + [(i, i + 1) for i in range(2, lags - 1)])
    load = base_2 + from_next.astype(jnp.float32) + part
    third, block_state = settle_friction(load, block_state, *block_columns)

    last = jnp.where(me == 0, third, jnp.where(me == 2, first, moved))
    below_v, above_v = exchange(last, every)
    change = block_state - before
    mine = change[:rows]
    for d in range(1, lags):
        piece = lax.ppermute(change[d * rows : (d + 1) * rows], "lag", [(0, d)])
        mine = jnp.where(me == d, piece, mine)
    state = state + mine
    traction = scatter_sum(product(meta, tile, below_v, last, above_v, lags))
    rates, state = settle_friction(stress + traction, state, *columns)
    return rates[None, None], state[None, None]


def solution(mesh):
    in_specs = (
        P("lag", "elem", None),
        P("lag", "elem", None),
        P("lag"),
        P("lag", "elem", None),
        P("elem", "lag", None, None),
        P("elem", "lag", None, None),
        P("elem", "lag", None),
        P("elem", "lag", None),
        P("elem", "lag", None),
    )
    out_specs = (P("elem", "lag", None, None), P("elem", "lag", None, None))
    return jax.shard_map(shards, mesh=mesh, in_specs=in_specs, out_specs=out_specs, check_vma=False)
```

```python
import functools

import jax
import jax.numpy as jnp
from jax import lax
from jax.experimental import pallas as pl
from jax.experimental.pallas import tpu as pltpu
from jax.sharding import PartitionSpec as P


NEWTON = 3


damping = 0.5
time_step = 0.25
creep_square = 0.01


def exchange(value, planes):
    count = lax.axis_size("elem")
    up = [(i * count + j, i * count + j + 1) for i in planes for j in range(count - 1)]
    down = [(j, i) for i, j in up]
    axes = ("lag", "elem")
    return lax.ppermute(value, axes, up), lax.ppermute(value, axes, down)


def fetch(meta, below, own, above, sources, sems):
    slots = sems.shape[0]
    block = sources.shape[0] // slots
    per = own.shape[0] // block
    live = meta[slots]

    for k in range(slots):
        spot = sources.at[pl.ds(k * block, block)]
        pick = meta[k]
        start = pl.multiple_of(lax.rem(pick, per) * block, block)
        for which, ref in enumerate((below, own, above)):

            @pl.when((k < live) & (lax.div(pick, per) == which))
            def _():
                pltpu.make_async_copy(ref.at[pl.ds(start, block)], spot, sems.at[k]).start()

        @pl.when(k >= live)
        def _():
            spot[...] = jnp.zeros(spot.shape, spot.dtype)

    for k in range(slots):
        spot = sources.at[pl.ds(k * block, block)]

        @pl.when(k < live)
        def _():
            pltpu.make_async_copy(own.at[pl.ds(0, block)], spot, sems.at[k]).wait()


def product_kernel(lags, rows, meta, tile, below, own, above, *refs):
    outs, sources, sems = refs[:lags], refs[lags], refs[lags + 1]
    me = meta[sems.shape[0] + 1]
    fetch(meta, below, own, above, sources, sems)
    for d in range(lags):
        first = pl.multiple_of(lax.rem(me + d, lags) * rows, rows)
        part = jnp.dot(tile[pl.ds(first, rows), :], sources[...], preferred_element_type=jnp.float32)
        outs[d][...] = part.astype(outs[d].dtype)


def product(meta, tile, below, own, above, lags):
    rows, cols = own.shape[0] // lags, own.shape[1]
    slots = meta.shape[0] - 2
    kernel = functools.partial(product_kernel, lags, rows)
    kinds = [jnp.float32] + [jnp.bfloat16] * (lags - 1)
    return pl.pallas_call(
        kernel,
        grid_spec=pltpu.PrefetchScalarGridSpec(
            num_scalar_prefetch=1,
            grid=(1,),
            in_specs=[pl.BlockSpec(memory_space=pltpu.VMEM)] + [pl.BlockSpec(memory_space=pl.ANY)] * 3,
            out_specs=[pl.BlockSpec(memory_space=pltpu.VMEM)] * lags,
            scratch_shapes=[
                pltpu.VMEM((tile.shape[1], cols), jnp.bfloat16),
                pltpu.SemaphoreType.DMA((slots,)),
            ],
        ),
        out_shape=[jax.ShapeDtypeStruct((rows, cols), kind) for kind in kinds],
        compiler_params=pltpu.CompilerParams(vmem_limit_bytes=24 * 1024 * 1024),
        cost_estimate=pl.CostEstimate(
            flops=2 * tile.size * cols, bytes_accessed=2 * (tile.size + 4 * own.size), transcendentals=0
        ),
        name="product",
    )(meta, tile, below, own, above)


def scatter_sum(parts):
    lags = len(parts)
    total = parts[0]
    for d in range(1, lags):
        route = [(i, (i + d) % lags) for i in range(lags)]
        total = total + lax.ppermute(parts[d], "lag", route).astype(jnp.float32)
    return total


def settle_friction(shear_load, state_now, coef_a, coef_b, sigma):
    scale = 0.5 * jnp.exp(coef_b / coef_a * state_now)
    strength = sigma * coef_a
    velocity = shear_load / (strength * scale + damping)
    for _ in range(NEWTON):
        scaled = scale * velocity
        magnitude = jnp.abs(scaled)
        root = jnp.sqrt(magnitude * magnitude + 1.0)
        positive = jnp.log(magnitude + root)
        arc = jnp.where(scaled < 0.0, -positive, positive)
        residual = strength * arc + damping * velocity - shear_load
        derivative = strength * scale / root + damping
        velocity = velocity - residual / derivative
    speed = jnp.sqrt(velocity * velocity + creep_square)
    new_state = state_now + time_step * (jnp.exp(-state_now) - speed)
    return velocity.astype(jnp.bfloat16), new_state


def full_product_kernel(chunks, meta, tile, below, own, above, stress, *refs):
    outs, sources, sems = refs[:-2], refs[-2], refs[-1]
    slots = sems.shape[0]
    me, active = meta[slots + 1], meta[slots + 2] > 0
    rows = outs[0].shape[0] // chunks
    mine = pl.ds(pl.multiple_of(me * stress.shape[0], stress.shape[0]), stress.shape[0])

    @pl.when(active)
    def _():
        fetch(meta, below, own, above, sources, sems)
        for d in range(chunks):
            spot = pl.ds(d * rows, rows)
            part = jnp.dot(tile[spot, :], sources[...], preferred_element_type=jnp.float32)
            for out in outs:
                out[spot, :] = part.astype(out.dtype)
        part = jnp.dot(tile[mine, :], sources[...], preferred_element_type=jnp.float32)
        outs[0][mine, :] = (part + stress[...]).astype(outs[0].dtype)

    @pl.when(jnp.logical_not(active))
    def _():
        outs[0][...] = jnp.zeros(outs[0].shape, outs[0].dtype)
        outs[0][mine, :] = stress[...].astype(outs[0].dtype)


def full_product(meta, active, tile, below, own, above, stress, kinds):
    slots = meta.shape[0] - 2
    meta = jnp.concatenate([meta, active.astype(jnp.int32)[None]])
    chunks = tile.shape[0] // min(tile.shape[0], 256)
    return pl.pallas_call(
        functools.partial(full_product_kernel, chunks),
        grid_spec=pltpu.PrefetchScalarGridSpec(
            num_scalar_prefetch=1,
            grid=(1,),
            in_specs=[pl.BlockSpec(memory_space=pltpu.VMEM)]
            + [pl.BlockSpec(memory_space=pl.ANY)] * 3
            + [pl.BlockSpec(memory_space=pltpu.VMEM)],
            out_specs=[pl.BlockSpec(memory_space=pltpu.VMEM)] * len(kinds),
            scratch_shapes=[pltpu.VMEM((tile.shape[1], own.shape[1]), jnp.bfloat16), pltpu.SemaphoreType.DMA((slots,))],
        ),
        out_shape=[jax.ShapeDtypeStruct(own.shape, kind) for kind in kinds],
        compiler_params=pltpu.CompilerParams(vmem_limit_bytes=24 * 1024 * 1024),
        cost_estimate=pl.CostEstimate(
            flops=2 * tile.size * own.shape[1], bytes_accessed=2 * (tile.size + 5 * own.size), transcendentals=0
        ),
        name="full_product",
    )(meta, tile, below, own, above, stress)


def tree_to_first(value, lags, least):
    stride = 1
    while stride < lags:
        route = [(i + stride, i) for i in range(0, lags - stride, 2 * stride) if i + stride >= least]
        added = lax.ppermute(value, "lag", route)
        value = lax.optimization_barrier(value.astype(jnp.float32) + added.astype(jnp.float32))
        stride *= 2
        if stride < lags:
            value = value.astype(jnp.bfloat16)
    return value


def shards(kernel_tiles, shell_index, cone_blocks, history, prestress, log_state, fric_a, fric_b, normal_stress):
    lags = lax.axis_size("lag")
    me = lax.axis_index("lag")
    every = range(lags)
    tile, field = kernel_tiles[0], history[0]
    rows = prestress.shape[2]
    meta = jnp.concatenate([shell_index[0, 0], cone_blocks, me[None].astype(jnp.int32)])
    stress, state = prestress[0, 0], log_state[0, 0]
    coefs = [fric_a[0, 0], fric_b[0, 0], normal_stress[0, 0]]
    columns = [c[:, None] for c in coefs]

    below, above = exchange(field, every)
    shifted = lax.ppermute(field, "lag", [(i, i + 1) for i in range(lags - 1)])
    packed = jnp.concatenate([state, jnp.pad(jnp.stack(coefs), ((0, 5), (0, state.shape[1] - rows)))], 0)
    gathered = [packed] + [lax.ppermute(packed, "lag", [(d, 0)]) for d in range(1, lags)]
    parts = product(meta, tile, below, field, above, lags)
    traction = scatter_sum(parts)
    rates, state = settle_friction(stress + traction, state, *columns)

    below_1, above_1 = exchange(shifted, [i for i in every if i >= 1])
    (part,) = full_product(meta, me >= 1, tile, below_1, shifted, above_1, stress, [jnp.bfloat16])
    base_1 = tree_to_first(part, lags, 1)
    twice = lax.ppermute(shifted, "lag", [(i, i + 1) for i in range(1, lags - 1)])
    below_2, above_2 = exchange(twice, [i for i in every if i >= 2])
    (part,) = full_product(meta, me >= 2, tile, below_2, twice, above_2, stress, [jnp.bfloat16])
    base_2 = tree_to_first(part, lags, 2)

    block_state = jnp.concatenate([g[:rows] for g in gathered], 0)
    block_columns = [jnp.concatenate([g[rows + k, :rows] for g in gathered])[:, None] for k in range(3)]
    first = lax.all_gather(rates, "lag", axis=0, tiled=True)
    speed = jnp.sqrt(jnp.square(first.astype(jnp.float32)) + creep_square)
    block_state = block_state + time_step * (jnp.exp(-block_state) - speed)
    before = block_state

    below_v, above_v = exchange(first, [0, 1])
    kinds = [jnp.bfloat16, jnp.float32]
    sent, part = full_product(meta, me <= 1, tile, below_v, first, above_v, stress, kinds)
    from_next = lax.ppermute(sent, "lag", [(1, 0)])
    second, block_state = settle_friction(base_1 + part, block_state, *block_columns)
    below_v, above_v = exchange(second, [0])
    kinds = [jnp.bfloat16, jnp.float32]
    _, part = full_product(meta, me == 0, tile, below_v, second, above_v, stress, kinds)
    sent = jnp.where(me == 0, second, twice)
    moved = lax.ppermute(sent, "lag", [(0, 1)] + [(i, i + 1) for i in range(2, lags - 1)])
    load = base_2 + from_next.astype(jnp.float32) + part
    third, block_state = settle_friction(load, block_state, *block_columns)

    last = jnp.where(me == 0, third, jnp.where(me == 2, first, moved))
    below_v, above_v = exchange(last, every)
    change = block_state - before
    mine = change[:rows]
    for d in range(1, lags):
        piece = lax.ppermute(change[d * rows : (d + 1) * rows], "lag", [(0, d)])
        mine = jnp.where(me == d, piece, mine)
    state = state + mine
    parts = product(meta, tile, below_v, last, above_v, lags)
    traction = scatter_sum(parts)
    rates, state = settle_friction(stress + traction, state, *columns)
    return rates[None, None], state[None, None]


def solution(mesh):
    in_specs = (
        P("lag", "elem", None),
        P("lag", "elem", None),
        P("lag"),
        P("lag", "elem", None),
        P("elem", "lag", None, None),
        P("elem", "lag", None, None),
        P("elem", "lag", None),
        P("elem", "lag", None),
        P("elem", "lag", None),
    )
    out_specs = (P("elem", "lag", None, None), P("elem", "lag", None, None))
    return jax.shard_map(shards, mesh=mesh, in_specs=in_specs, out_specs=out_specs, check_vma=False)
```

```python
import functools

import jax
import jax.numpy as jnp
from jax import lax
from jax.experimental import pallas as pl
from jax.experimental.pallas import tpu as pltpu
from jax.sharding import PartitionSpec as P


NEWTON = 3

damping = 0.5
time_step = 0.25
creep_square = 0.01

HBM = pl.BlockSpec(memory_space=pltpu.HBM)
VMEM = pl.BlockSpec(memory_space=pltpu.VMEM)
PARAMS = pltpu.CompilerParams(vmem_limit_bytes=32 * 1024 * 1024)


def exchange(value, planes):
    count = lax.axis_size("elem")
    up = [(i * count + j, i * count + j + 1) for i in planes for j in range(count - 1)]
    down = [(j, i) for i, j in up]
    axes = ("lag", "elem")
    return lax.ppermute(value, axes, up), lax.ppermute(value, axes, down)


class Operands:
    def __init__(self, picks, live, tile, below, own, above, starts, rows, tile_buf, sources, tile_sems, sems):
        slots = sems.shape[0]
        block = sources.shape[0] // slots
        per = own.shape[0] // block
        self.sources, self.tile_buf, self.rows = sources, tile_buf, rows
        alive = live[0]
        for k in range(slots):
            spot = sources.at[pl.ds(k * block, block)]
            pick = picks[0, 0, k]
            start = pl.multiple_of(lax.rem(pick, per) * block, block)
            for which, ref in enumerate((below, own, above)):

                @pl.when((k < alive) & (lax.div(pick, per) == which))
                def _():
                    pltpu.make_async_copy(ref.at[pl.ds(start, block)], spot, sems.at[k]).start()

        self.copies = []
        for d, start in enumerate(starts):
            spot = pl.ds(d * rows, rows)
            copy = pltpu.make_async_copy(tile.at[0, pl.ds(start, rows)], tile_buf.at[spot], tile_sems.at[d])
            copy.start()
            self.copies.append(copy)
        for k in range(slots):
            spot = sources.at[pl.ds(k * block, block)]

            @pl.when(k >= alive)
            def _():
                spot[...] = jnp.zeros(spot.shape, spot.dtype)

            @pl.when(k < alive)
            def _():
                pltpu.make_async_copy(own.at[pl.ds(0, block)], spot, sems.at[k]).wait()

    def chunk(self, d):
        self.copies[d].wait()
        spot = pl.ds(d * self.rows, self.rows)
        return jnp.dot(self.tile_buf[spot, :], self.sources[...], preferred_element_type=jnp.float32)


def scratch(tile, own, chunks, slots):
    return [
        pltpu.VMEM(tile.shape[1:], tile.dtype),
        pltpu.VMEM((tile.shape[2], own.shape[1]), own.dtype),
        pltpu.SemaphoreType.DMA((chunks,)),
        pltpu.SemaphoreType.DMA((slots,)),
    ]


def cost(tile, own, parts=0):
    return pl.CostEstimate(
        flops=2 * tile.size * own.shape[1],
        bytes_accessed=2 * (tile.size + 4 * own.size),
        transcendentals=parts * own.size,
    )


def rows_kernel(lags, rows, picks, live, tile, below, own, above, *refs):
    outs, bufs = refs[:lags], refs[lags:]
    me = lax.axis_index("lag")
    starts = [pl.multiple_of(lax.rem(me + d, lags) * rows, rows) for d in range(lags)]
    operands = Operands(picks, live, tile, below, own, above, starts, rows, *bufs)
    for d in range(lags):
        outs[d][...] = operands.chunk(d).astype(outs[d].dtype)


def product_by_rows(picks, live, tile, below, own, above, lags):
    rows = own.shape[0] // lags
    kinds = [jnp.float32] + [jnp.bfloat16] * (lags - 1)
    return pl.pallas_call(
        functools.partial(rows_kernel, lags, rows),
        grid_spec=pltpu.PrefetchScalarGridSpec(
            num_scalar_prefetch=2,
            grid=(1,),
            in_specs=[HBM] * 4,
            out_specs=[VMEM] * lags,
            scratch_shapes=scratch(tile, own, lags, picks.shape[2]),
        ),
        out_shape=[jax.ShapeDtypeStruct((rows, own.shape[1]), kind) for kind in kinds],
        compiler_params=PARAMS,
        cost_estimate=cost(tile, own),
        name="product_by_rows",
    )(picks, live, tile, below, own, above)


def later_kernel(chunks, picks, live, tile, below, own, above, stress, out, *bufs):
    me = lax.axis_index("lag")
    rows = out.shape[0] // chunks

    @pl.when(me > 0)
    def _():
        operands = Operands(
            picks, live, tile, below, own, above, [d * rows for d in range(chunks)], rows, *bufs
        )
        for d in range(chunks):
            out[pl.ds(d * rows, rows), :] = operands.chunk(d).astype(out.dtype)
        height = stress.shape[2]
        mine = pl.ds(pl.multiple_of(me * height, height), height)
        part = jnp.dot(bufs[0][mine, :], bufs[1][...], preferred_element_type=jnp.float32)
        out[mine, :] = (part + stress[0, 0]).astype(out.dtype)


def later_product(picks, live, tile, below, own, above, stress):
    chunks = max(1, tile.shape[1] // 256)
    return pl.pallas_call(
        functools.partial(later_kernel, chunks),
        grid_spec=pltpu.PrefetchScalarGridSpec(
            num_scalar_prefetch=2,
            grid=(1,),
            in_specs=[HBM] * 4 + [VMEM],
            out_specs=VMEM,
            scratch_shapes=scratch(tile, own, chunks, picks.shape[2]),
        ),
        out_shape=jax.ShapeDtypeStruct(own.shape, jnp.bfloat16),
        compiler_params=PARAMS,
        cost_estimate=cost(tile, own),
        name="later_product",
    )(picks, live, tile, below, own, above, stress)


def pack_kernel(state, coef_a, coef_b, sigma, out):
    rows = state.shape[2]
    out[pl.ds(0, rows), :] = state[0, 0]
    out[pl.ds(rows, 8), :] = jnp.zeros((8, out.shape[1]), out.dtype)
    out[pl.ds(rows, 1), pl.ds(0, rows)] = coef_b[0] / coef_a[0]
    out[pl.ds(rows + 1, 1), pl.ds(0, rows)] = sigma[0] * coef_a[0]


def pack(state, coef_a, coef_b, sigma):
    return pl.pallas_call(
        pack_kernel,
        in_specs=[VMEM] * 4,
        out_specs=VMEM,
        out_shape=jax.ShapeDtypeStruct((state.shape[2] + 8, state.shape[3]), jnp.float32),
        compiler_params=PARAMS,
        name="pack",
    )(state, coef_a, coef_b, sigma)


def newton(load, state, ratio, strength):
    scale = 0.5 * jnp.exp(ratio * state)
    product = strength * scale
    velocity = load / (product + damping)
    for _ in range(NEWTON):
        scaled = scale * velocity
        magnitude = jnp.abs(scaled)
        root = jnp.sqrt(magnitude * magnitude + 1.0)
        positive = jnp.log(magnitude + root)
        arc = jnp.where(scaled < 0.0, -positive, positive)
        residual = strength * arc + damping * velocity - load
        velocity = velocity - residual / (product / root + damping)
    return velocity


def evolved(state, speed_of):
    return state + time_step * (jnp.exp(-state) - jnp.sqrt(speed_of * speed_of + creep_square))


def step_kernel(lags, count, fresh, picks, live, tile, below, own, above, stress, *refs):
    received, refs = refs[:count], refs[count:]
    packed, refs = refs[:lags], refs[lags:]
    before, refs = refs[0], refs[1:]
    rates, after, loads, columns = refs[:4]
    bufs = refs[4:]
    rows = rates.shape[0] // lags
    group = min(32, rows)

    @pl.when(lax.axis_index("lag") == 0)
    def _():
        operands = Operands(picks, live, tile, below, own, above, [d * rows for d in range(lags)], rows, *bufs)
        for d in range(lags):
            params = packed[d][pl.ds(rows, 8), :] if fresh else packed[d][...]
            columns[...] = jnp.transpose(params)
            loads[...] = operands.chunk(d)
            if d == 0:
                loads[...] += stress[0, 0]

            @pl.loop(0, rows // group)
            def _(i):
                part = pl.ds(pl.multiple_of(i * group, group), group)
                whole = pl.ds(pl.multiple_of(d * rows + i * group, group), group)
                load = loads[part, :]
                for ref in received:
                    load = load + ref[whole, :].astype(jnp.float32)
                if fresh:
                    state = evolved(packed[d][part, :], before[whole, :].astype(jnp.float32))
                else:
                    state = before[whole, :]
                both = columns[part, :]
                velocity = newton(load, state, both[:, 0:1], both[:, 1:2])
                rates[whole, :] = velocity.astype(rates.dtype)
                after[whole, :] = evolved(state, velocity)


def plane_step(picks, live, tile, below, own, above, stress, received, packed, before):
    lags, fresh = len(packed), before is None
    rows, cols = own.shape[0] // lags, own.shape[1]
    kernel = functools.partial(step_kernel, lags, len(received), fresh)
    param = VMEM if fresh else pl.BlockSpec((8, cols), lambda i, *_: (rows // 8, 0))
    more = [own] if fresh else [before]
    return pl.pallas_call(
        kernel,
        grid_spec=pltpu.PrefetchScalarGridSpec(
            num_scalar_prefetch=2,
            grid=(1,),
            in_specs=[HBM] * 4 + [VMEM] * (1 + len(received)) + [param] * lags + [VMEM],
            out_specs=[VMEM] * 2,
            scratch_shapes=[pltpu.VMEM((rows, cols), jnp.float32), pltpu.VMEM((cols, 8), jnp.float32)]
            + scratch(tile, own, lags, picks.shape[2]),
        ),
        out_shape=[jax.ShapeDtypeStruct(own.shape, jnp.bfloat16), jax.ShapeDtypeStruct(own.shape, jnp.float32)],
        compiler_params=PARAMS,
        cost_estimate=cost(tile, own, 10),
        name="plane_step",
    )(picks, live, tile, below, own, above, stress, *received, *packed, *more)


def scatter_sum(parts):
    lags = len(parts)
    total = parts[0]
    for d in range(1, lags):
        route = [(i, (i + d) % lags) for i in range(lags)]
        total = total + lax.ppermute(parts[d], "lag", route).astype(jnp.float32)
    return total


def tree_to_first(value, lags):
    received, stride = [], 1
    while stride < lags:
        route = [(i + stride, i) for i in range(0, lags - stride, 2 * stride)]
        received.append(lax.ppermute(value, "lag", route))
        stride *= 2
        if stride < lags:
            total = value.astype(jnp.float32) + received[-1].astype(jnp.float32)
            value = lax.optimization_barrier(total.astype(jnp.bfloat16))
    return received


def settle_friction(shear_load, state, coef_a, coef_b, sigma):
    velocity = newton(shear_load, state, coef_b / coef_a, sigma * coef_a)
    return velocity.astype(jnp.bfloat16), evolved(state, velocity)


def shards(kernel_tiles, shell_index, cone_blocks, history, prestress, log_state, fric_a, fric_b, normal_stress):
    lags = lax.axis_size("lag")
    me = lax.axis_index("lag")
    every = range(lags)
    local = (shell_index, cone_blocks, kernel_tiles)
    field = history[0]
    rows = prestress.shape[2]
    columns = [c[0, 0][:, None] for c in (fric_a, fric_b, normal_stress)]

    below, above = exchange(field, every)
    shifted = lax.ppermute(field, "lag", [(i, i + 1) for i in range(lags - 1)])
    packed = pack(log_state, fric_a, fric_b, normal_stress)
    packed = [packed] + [lax.ppermute(packed, "lag", [(d, 0)]) for d in range(1, lags)]
    traction = scatter_sum(product_by_rows(*local, below, field, above, lags))
    rates, _ = settle_friction(prestress[0, 0] + traction, log_state[0, 0], *columns)

    below, above = exchange(shifted, [i for i in every if i >= 1])
    base_1 = tree_to_first(later_product(*local, below, shifted, above, prestress), lags)
    twice = lax.ppermute(shifted, "lag", [(i, i + 1) for i in range(1, lags - 1)])

    first = lax.all_gather(rates, "lag", axis=0, tiled=True)
    source = jnp.where(me <= 1, first, twice)
    below, above = exchange(source, every)
    base_2 = tree_to_first(later_product(*local, below, source, above, prestress), lags)
    second, state = plane_step(*local, below, source, above, prestress, base_1, packed, None)
    below, above = exchange(second, [0])
    moved = jnp.where(me == 0, second, twice)
    moved = lax.ppermute(moved, "lag", [(0, 1)] + [(i, i + 1) for i in range(2, lags - 1)])
    third, state = plane_step(*local, below, second, above, prestress, base_2, packed, state)

    last = jnp.where(me == 0, third, jnp.where(me == 2, first, moved))
    below, above = exchange(last, every)
    mine = state[:rows]
    for d in range(1, lags):
        piece = lax.ppermute(state[d * rows : (d + 1) * rows], "lag", [(0, d)])
        mine = jnp.where(me == d, piece, mine)
    traction = scatter_sum(product_by_rows(*local, below, last, above, lags))
    rates, state = settle_friction(prestress[0, 0] + traction, mine, *columns)
    return rates[None, None], state[None, None]


def solution(mesh):
    in_specs = (
        P("lag", "elem", None),
        P("lag", "elem", None),
        P("lag"),
        P("lag", "elem", None),
        P("elem", "lag", None, None),
        P("elem", "lag", None, None),
        P("elem", "lag", None),
        P("elem", "lag", None),
        P("elem", "lag", None),
    )
    out_specs = (P("elem", "lag", None, None), P("elem", "lag", None, None))
    return jax.shard_map(shards, mesh=mesh, in_specs=in_specs, out_specs=out_specs, check_vma=False)
```

```python
import functools

import jax
import jax.numpy as jnp
from jax import lax
from jax.experimental import pallas as pl
from jax.experimental.pallas import tpu as pltpu
from jax.sharding import PartitionSpec as P


STEPS = 4
NEWTON = 3

damping = 0.5
time_step = 0.25
creep_square = 0.01

ANY = pl.BlockSpec(memory_space=pl.ANY)
VMEM = pl.BlockSpec(memory_space=pltpu.VMEM)
PARAMS = pltpu.CompilerParams(vmem_limit_bytes=32 * 1024 * 1024)


def exchange(value, planes):
    count = lax.axis_size("elem")
    up = [(i * count + j, i * count + j + 1) for i in planes for j in range(count - 1)]
    down = [(j, i) for i, j in up]
    axes = ("lag", "elem")
    return lax.ppermute(value, axes, up), lax.ppermute(value, axes, down)


def fetch(picks, live, below, own, above, sources, sems):
    slots = sems.shape[0]
    block = sources.shape[0] // slots
    per = own.shape[0] // block
    alive = live[0]
    for k in range(slots):
        spot = sources.at[pl.ds(k * block, block)]
        pick = picks[0, 0, k]
        start = pl.multiple_of(lax.rem(pick, per) * block, block)
        for which, ref in enumerate((below, own, above)):

            @pl.when((k < alive) & (lax.div(pick, per) == which))
            def _():
                pltpu.make_async_copy(ref.at[pl.ds(start, block)], spot, sems.at[k]).start()

    for k in range(slots):
        spot = sources.at[pl.ds(k * block, block)]

        @pl.when(k >= alive)
        def _():
            spot[...] = jnp.zeros(spot.shape, spot.dtype)

        @pl.when(k < alive)
        def _():
            pltpu.make_async_copy(own.at[pl.ds(0, block)], spot, sems.at[k]).wait()


def rows_kernel(lags, rows, picks, live, tile, below, own, above, *refs):
    outs, sources, sems = refs[:lags], refs[lags], refs[lags + 1]
    me = lax.axis_index("lag")
    fetch(picks, live, below, own, above, sources, sems)
    for d in range(lags):
        first = pl.multiple_of(lax.rem(me + d, lags) * rows, rows)
        part = jnp.dot(tile[0, pl.ds(first, rows), :], sources[...], preferred_element_type=jnp.float32)
        outs[d][...] = part.astype(outs[d].dtype)


def product_by_rows(picks, live, tile, below, own, above, lags):
    rows, cols = own.shape[0] // lags, own.shape[1]
    kinds = [jnp.float32] + [jnp.bfloat16] * (lags - 1)
    return pl.pallas_call(
        functools.partial(rows_kernel, lags, rows),
        grid_spec=pltpu.PrefetchScalarGridSpec(
            num_scalar_prefetch=2,
            grid=(1,),
            in_specs=[VMEM] + [ANY] * 3,
            out_specs=[VMEM] * lags,
            scratch_shapes=[pltpu.VMEM((tile.shape[2], cols), own.dtype), pltpu.SemaphoreType.DMA((picks.shape[2],))],
        ),
        out_shape=[jax.ShapeDtypeStruct((rows, cols), kind) for kind in kinds],
        compiler_params=PARAMS,
        cost_estimate=pl.CostEstimate(
            flops=2 * tile.size * cols, bytes_accessed=2 * (tile.size + 4 * own.size), transcendentals=0
        ),
        name="product_by_rows",
    )(picks, live, tile, below, own, above)


def newton(load, state, ratio, strength):
    scale = 0.5 * jnp.exp(ratio * state)
    product = strength * scale
    velocity = load / (product + damping)
    for _ in range(NEWTON):
        scaled = scale * velocity
        magnitude = jnp.abs(scaled)
        root = jnp.sqrt(magnitude * magnitude + 1.0)
        positive = jnp.log(magnitude + root)
        arc = jnp.where(scaled < 0.0, -positive, positive)
        residual = strength * arc + damping * velocity - load
        velocity = velocity - residual / (product / root + damping)
    return velocity


def evolved(state, speed_of):
    return state + time_step * (jnp.exp(-state) - jnp.sqrt(speed_of * speed_of + creep_square))


def scatter_sum(parts):
    lags = len(parts)
    total = parts[0]
    for d in range(1, lags):
        route = [(i, (i + d) % lags) for i in range(lags)]
        total = total + lax.ppermute(parts[d], "lag", route).astype(jnp.float32)
    return total


def settle_friction(shear_load, state, coef_a, coef_b, sigma):
    velocity = newton(shear_load, state, coef_b / coef_a, sigma * coef_a)
    return velocity.astype(jnp.bfloat16), evolved(state, velocity)


def shards(kernel_tiles, shell_index, cone_blocks, history, prestress, log_state, fric_a, fric_b, normal_stress):
    lags = lax.axis_size("lag")
    me = lax.axis_index("lag")
    local = (shell_index, cone_blocks, kernel_tiles)
    field, state = history[0], log_state[0, 0]
    columns = [c[0, 0][:, None] for c in (fric_a, fric_b, normal_stress)]
    for step in range(STEPS):
        below, above = exchange(field, range(lags))
        if step + 1 < STEPS:
            older = lax.ppermute(field, "lag", [(i, i + 1) for i in range(lags - 1)])
        parts = product_by_rows(*local, below, field, above, lags)
        traction = scatter_sum(parts)
        rates, state = settle_friction(prestress[0, 0] + traction, state, *columns)
        if step + 1 < STEPS:
            newest = lax.all_gather(rates, "lag", axis=0, tiled=True)
            field = jnp.where(me == 0, newest, older)
    return rates[None, None], state[None, None]


def solution(mesh):
    in_specs = (
        P("lag", "elem", None),
        P("lag", "elem", None),
        P("lag"),
        P("lag", "elem", None),
        P("elem", "lag", None, None),
        P("elem", "lag", None, None),
        P("elem", "lag", None),
        P("elem", "lag", None),
        P("elem", "lag", None),
    )
    out_specs = (P("elem", "lag", None, None), P("elem", "lag", None, None))
    return jax.shard_map(shards, mesh=mesh, in_specs=in_specs, out_specs=out_specs, check_vma=False)
```

```python
import functools

import jax
import jax.numpy as jnp
from jax import lax
from jax.experimental import pallas as pl
from jax.experimental.pallas import tpu as pltpu
from jax.sharding import PartitionSpec as P


STEPS = 4
NEWTON = 3

damping = 0.5
time_step = 0.25
creep_square = 0.01

ANY = pl.BlockSpec(memory_space=pl.ANY)
VMEM = pl.BlockSpec(memory_space=pltpu.VMEM)
PARAMS = pltpu.CompilerParams(vmem_limit_bytes=32 * 1024 * 1024)


def exchange(value, planes):
    count = lax.axis_size("elem")
    up = [(i * count + j, i * count + j + 1) for i in planes for j in range(count - 1)]
    down = [(j, i) for i, j in up]
    axes = ("lag", "elem")
    return lax.ppermute(value, axes, up), lax.ppermute(value, axes, down)


def fetch(where, picks, live, refs, sources, sems):
    slots = sems.shape[0]
    block = sources.shape[0] // slots
    alive = live[0]
    for k in range(slots):
        spot = sources.at[pl.ds(k * block, block)]
        for p, (which, first) in enumerate(where):

            @pl.when((k < alive) & (picks[0, 0, k] == p))
            def _():
                pltpu.make_async_copy(refs[which].at[pl.ds(first, block)], spot, sems.at[k]).start()

    for k in range(slots):
        spot = sources.at[pl.ds(k * block, block)]

        @pl.when(k >= alive)
        def _():
            spot[...] = jnp.zeros(spot.shape, spot.dtype)

        @pl.when(k < alive)
        def _():
            pltpu.make_async_copy(refs[0].at[pl.ds(0, block)], spot, sems.at[k]).wait()


def rows_kernel(lags, rows, where, count, picks, live, tile, *refs):
    window, outs, sources, sems = refs[:count], refs[count : count + lags], refs[-2], refs[-1]
    me = lax.axis_index("lag")
    fetch(where, picks, live, window, sources, sems)
    for d in range(lags):
        first = pl.multiple_of(lax.rem(me + d, lags) * rows, rows)
        part = jnp.dot(tile[0, pl.ds(first, rows), :], sources[...], preferred_element_type=jnp.float32)
        outs[d][...] = part.astype(outs[d].dtype)


def product_by_rows(picks, live, tile, window, lags):
    rows, cols = tile.shape[1] // lags, window[0].shape[1]
    block = tile.shape[2] // picks.shape[2]
    where = [(i, first) for i, part in enumerate(window) for first in range(0, part.shape[0], block)]
    kinds = [jnp.float32] + [jnp.bfloat16] * (lags - 1)
    return pl.pallas_call(
        functools.partial(rows_kernel, lags, rows, where, len(window)),
        grid_spec=pltpu.PrefetchScalarGridSpec(
            num_scalar_prefetch=2,
            grid=(1,),
            in_specs=[VMEM] + [ANY] * len(window),
            out_specs=[VMEM] * lags,
            scratch_shapes=[
                pltpu.VMEM((tile.shape[2], cols), window[0].dtype),
                pltpu.SemaphoreType.DMA((picks.shape[2],)),
            ],
        ),
        out_shape=[jax.ShapeDtypeStruct((rows, cols), kind) for kind in kinds],
        compiler_params=PARAMS,
        cost_estimate=pl.CostEstimate(
            flops=2 * tile.size * cols,
            bytes_accessed=2 * (tile.size + sum(part.size for part in window)),
            transcendentals=0,
        ),
        name="product_by_rows",
    )(picks, live, tile, *window)


def newton(load, state, ratio, strength):
    scale = 0.5 * jnp.exp(ratio * state)
    product = strength * scale
    velocity = load / (product + damping)
    for _ in range(NEWTON):
        scaled = scale * velocity
        magnitude = jnp.abs(scaled)
        root = jnp.sqrt(magnitude * magnitude + 1.0)
        positive = jnp.log(magnitude + root)
        arc = jnp.where(scaled < 0.0, -positive, positive)
        residual = strength * arc + damping * velocity - load
        velocity = velocity - residual / (product / root + damping)
    return velocity


def evolved(state, speed_of):
    return state + time_step * (jnp.exp(-state) - jnp.sqrt(speed_of * speed_of + creep_square))


def scatter_sum(parts):
    lags = len(parts)
    total = parts[0]
    for d in range(1, lags):
        route = [(i, (i + d) % lags) for i in range(lags)]
        total = total + lax.ppermute(parts[d], "lag", route).astype(jnp.float32)
    return total


def settle_friction(shear_load, state, coef_a, coef_b, sigma):
    velocity = newton(shear_load, state, coef_b / coef_a, sigma * coef_a)
    return velocity.astype(jnp.bfloat16), evolved(state, velocity)


def shards(kernel_tiles, shell_index, cone_blocks, history, prestress, log_state, fric_a, fric_b, normal_stress):
    lags = lax.axis_size("lag")
    me = lax.axis_index("lag")
    local = (shell_index, cone_blocks, kernel_tiles)
    pieces, state = [history[0]], log_state[0, 0]
    parts = history.shape[1] * shell_index.shape[2] // kernel_tiles.shape[2]
    columns = [c[0, 0][:, None] for c in (fric_a, fric_b, normal_stress)]
    for step in range(STEPS):
        sides = [exchange(piece, range(lags)) for piece in pieces]
        window = [side[0] for side in sides] + pieces + [side[1] for side in sides]
        if step + 1 < STEPS:
            field = jnp.concatenate(pieces, 0)
            older = lax.ppermute(field, "lag", [(i, i + 1) for i in range(lags - 1)])
        traction = scatter_sum(product_by_rows(*local, window, lags))
        rates, state = settle_friction(prestress[0, 0] + traction, state, *columns)
        if step + 1 < STEPS:
            newest = [rates] + [lax.ppermute(rates, "lag", [(d, 0)]) for d in range(1, lags)]
            size, height = lags // parts, older.shape[0] // parts
            pieces, me_now = [], me
            for i in range(parts):
                new = jnp.concatenate(newest[i * size : (i + 1) * size], 0)
                piece = jnp.where(me_now == 0, new, older[i * height : (i + 1) * height])
                piece, older, me_now = lax.optimization_barrier((piece, older, me_now))
                pieces.append(piece)
    return rates[None, None], state[None, None]


def solution(mesh):
    in_specs = (
        P("lag", "elem", None),
        P("lag", "elem", None),
        P("lag"),
        P("lag", "elem", None),
        P("elem", "lag", None, None),
        P("elem", "lag", None, None),
        P("elem", "lag", None),
        P("elem", "lag", None),
        P("elem", "lag", None),
    )
    out_specs = (P("elem", "lag", None, None), P("elem", "lag", None, None))
    return jax.shard_map(shards, mesh=mesh, in_specs=in_specs, out_specs=out_specs, check_vma=False)
```

```python
import functools

import jax
import jax.numpy as jnp
from jax import lax
from jax.experimental import pallas as pl
from jax.experimental.pallas import tpu as pltpu
from jax.sharding import PartitionSpec as P


STEPS = 4
NEWTON = 3

damping = 0.5
time_step = 0.25
creep_square = 0.01

ANY = pl.BlockSpec(memory_space=pl.ANY)
VMEM = pl.BlockSpec(memory_space=pltpu.VMEM)
PARAMS = pltpu.CompilerParams(vmem_limit_bytes=32 * 1024 * 1024)


def exchange(value, planes):
    count = lax.axis_size("elem")
    up = [(i * count + j, i * count + j + 1) for i in planes for j in range(count - 1)]
    down = [(j, i) for i, j in up]
    axes = ("lag", "elem")
    return lax.ppermute(value, axes, up), lax.ppermute(value, axes, down)


def fetch(windows, picks, live, sources, sems):
    slots = sems.shape[0]
    block = sources.shape[0] // slots
    alive = live[0]
    for k in range(slots):
        spot = sources.at[pl.ds(k * block, block)]
        pick = picks[0, 0, k]
        for holds, refs in windows:
            per = refs[1].shape[0] // block
            start = pl.multiple_of(lax.rem(pick, per) * block, block)
            for which, ref in enumerate(refs):

                @pl.when(holds & (k < alive) & (lax.div(pick, per) == which))
                def _():
                    pltpu.make_async_copy(ref.at[pl.ds(start, block)], spot, sems.at[k]).start()

    for k in range(slots):
        spot = sources.at[pl.ds(k * block, block)]

        @pl.when(k >= alive)
        def _():
            spot[...] = jnp.zeros(spot.shape, spot.dtype)

        @pl.when(k < alive)
        def _():
            pltpu.make_async_copy(windows[0][1][1].at[pl.ds(0, block)], spot, sems.at[k]).wait()


def rows_kernel(lags, rows, least, count, picks, live, tile, *refs):
    window, outs, sources, sems = refs[: 3 * count], refs[3 * count : 3 * count + lags], refs[-2], refs[-1]
    me = lax.axis_index("lag")
    windows = [window[3 * i : 3 * i + 3] for i in range(count)]
    holds = [me == least + i for i in range(count - 1)] + [me >= least + count - 1]

    @pl.when(me >= least)
    def _():
        fetch(list(zip(holds, windows)), picks, live, sources, sems)
        for d in range(lags):
            first = pl.multiple_of(lax.rem(me + d, lags) * rows, rows)
            part = jnp.dot(tile[0, pl.ds(first, rows), :], sources[...], preferred_element_type=jnp.float32)
            outs[d][...] = part.astype(outs[d].dtype)

    if least:

        @pl.when(me < least)
        def _():
            outs[0][...] = jnp.zeros(outs[0].shape, outs[0].dtype)


def product_by_rows(picks, live, tile, least, windows, lags):
    rows, cols = tile.shape[1] // lags, windows[0][0].shape[1]
    kinds = [jnp.float32] + [jnp.bfloat16] * (lags - 1)
    return pl.pallas_call(
        functools.partial(rows_kernel, lags, rows, least, len(windows)),
        grid_spec=pltpu.PrefetchScalarGridSpec(
            num_scalar_prefetch=2,
            grid=(1,),
            in_specs=[VMEM] + [ANY] * (3 * len(windows)),
            out_specs=[VMEM] * lags,
            scratch_shapes=[
                pltpu.VMEM((tile.shape[2], cols), windows[0][0].dtype),
                pltpu.SemaphoreType.DMA((picks.shape[2],)),
            ],
        ),
        out_shape=[jax.ShapeDtypeStruct((rows, cols), kind) for kind in kinds],
        compiler_params=PARAMS,
        cost_estimate=pl.CostEstimate(
            flops=2 * tile.size * cols, bytes_accessed=2 * (tile.size + 4 * rows * lags * cols), transcendentals=0
        ),
        name="product_by_rows",
    )(picks, live, tile, *[part for window in windows for part in window])


def own_kernel(lags, picks, live, tile, *refs):
    moved, window, out = refs[: lags - 1], refs[lags - 1 : lags + 2], refs[lags + 2]
    mine, sources, tile_sem, sems = refs[lags + 3 :]
    me = lax.axis_index("lag")
    rows = mine.shape[0]
    for d, ref in enumerate([tile.at[0, pl.ds(0, rows)], *moved]):

        @pl.when(me == d)
        def _():
            pltpu.make_async_copy(ref, mine, tile_sem).start()

    fetch([(me >= 0, window)], picks, live, sources, sems)
    pltpu.make_async_copy(tile.at[0, pl.ds(0, rows)], mine, tile_sem).wait()
    out[...] = jnp.dot(mine[...], sources[...], preferred_element_type=jnp.float32)


def own_product(picks, live, tile, moved, window):
    rows, cols = moved[0].shape[0], window[0].shape[1]
    return pl.pallas_call(
        functools.partial(own_kernel, len(moved) + 1),
        grid_spec=pltpu.PrefetchScalarGridSpec(
            num_scalar_prefetch=2,
            grid=(1,),
            in_specs=[ANY] * (4 + len(moved)),
            out_specs=VMEM,
            scratch_shapes=[
                pltpu.VMEM(moved[0].shape, tile.dtype),
                pltpu.VMEM((tile.shape[2], cols), window[0].dtype),
                pltpu.SemaphoreType.DMA(()),
                pltpu.SemaphoreType.DMA((picks.shape[2],)),
            ],
        ),
        out_shape=jax.ShapeDtypeStruct((rows, cols), jnp.float32),
        compiler_params=PARAMS,
        cost_estimate=pl.CostEstimate(
            flops=2 * moved[0].size * cols, bytes_accessed=2 * (moved[0].size + 3 * window[0].size), transcendentals=0
        ),
        name="own_product",
    )(picks, live, tile, *moved, *window)


def newton(load, state, ratio, strength):
    scale = 0.5 * jnp.exp(ratio * state)
    product = strength * scale
    velocity = load / (product + damping)
    for _ in range(NEWTON):
        scaled = scale * velocity
        magnitude = jnp.abs(scaled)
        root = jnp.sqrt(magnitude * magnitude + 1.0)
        positive = jnp.log(magnitude + root)
        arc = jnp.where(scaled < 0.0, -positive, positive)
        residual = strength * arc + damping * velocity - load
        velocity = velocity - residual / (product / root + damping)
    return velocity


def evolved(state, speed_of):
    return state + time_step * (jnp.exp(-state) - jnp.sqrt(speed_of * speed_of + creep_square))


def scatter_sum(parts, least):
    lags = len(parts)
    total = parts[0]
    for d in range(1, lags):
        route = [(i, (i + d) % lags) for i in range(least, lags)]
        total = total + lax.ppermute(parts[d], "lag", route).astype(jnp.float32)
    return total


def settle_friction(shear_load, state, coef_a, coef_b, sigma):
    velocity = newton(shear_load, state, coef_b / coef_a, sigma * coef_a)
    return velocity.astype(jnp.bfloat16), evolved(state, velocity)


def shards(kernel_tiles, shell_index, cone_blocks, history, prestress, log_state, fric_a, fric_b, normal_stress):
    lags = lax.axis_size("lag")
    local = (shell_index, cone_blocks, kernel_tiles)
    field, state, rows = history[0], log_state[0, 0], prestress.shape[2]
    columns = [c[0, 0][:, None] for c in (fric_a, fric_b, normal_stress)]

    def window_of(own, least):
        below, above = exchange(own, range(least, lags))
        return below, own, above

    window = window_of(field, 0)
    shifted = lax.ppermute(field, "lag", [(i, i + 1) for i in range(lags - 1)])
    moved = [lax.ppermute(kernel_tiles[0, d * rows : (d + 1) * rows], "lag", [(0, d)]) for d in range(1, lags)]
    table = jnp.concatenate([shell_index[0, 0], cone_blocks])
    table = lax.all_gather(table, "lag", axis=0, tiled=False)[0]
    newest = (table[None, None, :-1], table[-1:], kernel_tiles, moved)
    traction = scatter_sum(product_by_rows(*local, 0, [window], lags), 0)
    rates, state = settle_friction(prestress[0, 0] + traction, state, *columns)

    known = []
    for step in range(1, STEPS):
        windows = known + [window_of(shifted, step)]
        first = lax.all_gather(rates, "lag", axis=0, tiled=True)
        window = window_of(first, 0)
        parts = product_by_rows(*local, 1, windows, lags)
        traction = scatter_sum(parts, 1)
        if step + 1 < STEPS:
            shifted = lax.ppermute(shifted, "lag", [(i, i + 1) for i in range(step, lags - 1)])
        traction = traction + own_product(*newest, window)
        rates, state = settle_friction(prestress[0, 0] + traction, state, *columns)
        known = [window] + known
    return rates[None, None], state[None, None]


def solution(mesh):
    in_specs = (
        P("lag", "elem", None),
        P("lag", "elem", None),
        P("lag"),
        P("lag", "elem", None),
        P("elem", "lag", None, None),
        P("elem", "lag", None, None),
        P("elem", "lag", None),
        P("elem", "lag", None),
        P("elem", "lag", None),
    )
    out_specs = (P("elem", "lag", None, None), P("elem", "lag", None, None))
    return jax.shard_map(shards, mesh=mesh, in_specs=in_specs, out_specs=out_specs, check_vma=False)
```

```python
import functools

import jax
import jax.numpy as jnp
from jax import lax
from jax.experimental import pallas as pl
from jax.experimental.pallas import tpu as pltpu
from jax.sharding import PartitionSpec as P


NEWTON = 3

damping = 0.5
time_step = 0.25
creep_square = 0.01

ANY = pl.BlockSpec(memory_space=pl.ANY)
VMEM = pl.BlockSpec(memory_space=pltpu.VMEM)
PARAMS = pltpu.CompilerParams(vmem_limit_bytes=32 * 1024 * 1024)


def exchange(value, planes):
    count = lax.axis_size("elem")
    up = [(i * count + j, i * count + j + 1) for i in planes for j in range(count - 1)]
    down = [(j, i) for i, j in up]
    axes = ("lag", "elem")
    return lax.ppermute(value, axes, up), lax.ppermute(value, axes, down)


def fetch(picks, live, below, own, above, sources, sems):
    slots = sems.shape[0]
    block = sources.shape[0] // slots
    per = own.shape[0] // block
    alive = live[0]
    for k in range(slots):
        spot = sources.at[pl.ds(k * block, block)]
        pick = picks[0, 0, k]
        start = pl.multiple_of(lax.rem(pick, per) * block, block)
        for which, ref in enumerate((below, own, above)):

            @pl.when((k < alive) & (lax.div(pick, per) == which))
            def _():
                pltpu.make_async_copy(ref.at[pl.ds(start, block)], spot, sems.at[k]).start()

    for k in range(slots):
        spot = sources.at[pl.ds(k * block, block)]

        @pl.when(k >= alive)
        def _():
            spot[...] = jnp.zeros(spot.shape, spot.dtype)

        @pl.when(k < alive)
        def _():
            pltpu.make_async_copy(own.at[pl.ds(0, block)], spot, sems.at[k]).wait()


def rows_kernel(lags, rows, picks, live, tile, below, own, above, *refs):
    outs, sources, sems = refs[:lags], refs[lags], refs[lags + 1]
    me = lax.axis_index("lag")
    fetch(picks, live, below, own, above, sources, sems)
    for d in range(lags):
        first = pl.multiple_of(lax.rem(me + d, lags) * rows, rows)
        part = jnp.dot(tile[0, pl.ds(first, rows), :], sources[...], preferred_element_type=jnp.float32)
        outs[d][...] = part.astype(outs[d].dtype)


def product_by_rows(picks, live, tile, below, own, above, lags):
    rows, cols = own.shape[0] // lags, own.shape[1]
    kinds = [jnp.float32] + [jnp.bfloat16] * (lags - 1)
    return pl.pallas_call(
        functools.partial(rows_kernel, lags, rows),
        grid_spec=pltpu.PrefetchScalarGridSpec(
            num_scalar_prefetch=2,
            grid=(1,),
            in_specs=[VMEM] + [ANY] * 3,
            out_specs=[VMEM] * lags,
            scratch_shapes=[pltpu.VMEM((tile.shape[2], cols), own.dtype), pltpu.SemaphoreType.DMA((picks.shape[2],))],
        ),
        out_shape=[jax.ShapeDtypeStruct((rows, cols), kind) for kind in kinds],
        compiler_params=PARAMS,
        cost_estimate=pl.CostEstimate(
            flops=2 * tile.size * cols, bytes_accessed=2 * (tile.size + 4 * own.size), transcendentals=0
        ),
        name="product_by_rows",
    )(picks, live, tile, below, own, above)


def block_kernel(chunks, planes, high_too, picks, live, tile, below, own, above, stress, *refs):
    outs, sources, sems = refs[:-2], refs[-2], refs[-1]
    me = lax.axis_index("lag")
    rows, height = own.shape[0] // chunks, stress.shape[2]
    mine = pl.ds(pl.multiple_of(me * height, height), height)

    def write(out):
        for d in range(chunks):
            spot = pl.ds(d * rows, rows)
            part = jnp.dot(tile[0, spot, :], sources[...], preferred_element_type=jnp.float32)
            out[spot, :] = part.astype(out.dtype)
        part = jnp.dot(tile[0, mine, :], sources[...], preferred_element_type=jnp.float32)
        out[mine, :] = (part + stress[0, 0]).astype(out.dtype)

    @pl.when((me >= planes[0]) & (me <= planes[-1]))
    def _():
        fetch(picks, live, below, own, above, sources, sems)
        if high_too:

            @pl.when(me == 0)
            def _():
                write(outs[0])

            @pl.when(me > 0)
            def _():
                write(outs[1])

        else:
            write(outs[0])


def block_product(picks, live, tile, window, stress, planes, kinds):
    below, own, above = window
    chunks = max(1, tile.shape[1] // 256)
    return pl.pallas_call(
        functools.partial(block_kernel, chunks, (planes[0], planes[-1]), len(kinds) > 1),
        grid_spec=pltpu.PrefetchScalarGridSpec(
            num_scalar_prefetch=2,
            grid=(1,),
            in_specs=[VMEM] + [ANY] * 3 + [VMEM],
            out_specs=[VMEM] * len(kinds),
            scratch_shapes=[
                pltpu.VMEM((tile.shape[2], own.shape[1]), own.dtype),
                pltpu.SemaphoreType.DMA((picks.shape[2],)),
            ],
        ),
        out_shape=[jax.ShapeDtypeStruct(own.shape, kind) for kind in kinds],
        compiler_params=PARAMS,
        cost_estimate=pl.CostEstimate(
            flops=2 * tile.size * own.shape[1], bytes_accessed=2 * (tile.size + 4 * own.size), transcendentals=0
        ),
        name="block_product",
    )(picks, live, tile, below, own, above, stress)


def pack_kernel(state, coef_a, coef_b, sigma, tile, field, out):
    rows = state.shape[2]
    out[pl.ds(0, rows), :] = state[0, 0]
    out[pl.ds(rows, 8), :] = jnp.zeros((8, out.shape[1]), out.dtype)
    out[pl.ds(rows, 1), pl.ds(0, rows)] = coef_b[0] / coef_a[0]
    out[pl.ds(rows + 1, 1), pl.ds(0, rows)] = sigma[0] * coef_a[0]


def pack(state, coef_a, coef_b, sigma, tile, field):
    return pl.pallas_call(
        pack_kernel,
        in_specs=[VMEM] * 4 + [ANY] * 2,
        out_specs=VMEM,
        out_shape=jax.ShapeDtypeStruct((state.shape[2] + 8, state.shape[3]), jnp.float32),
        compiler_params=PARAMS,
        name="pack",
    )(state, coef_a, coef_b, sigma, tile, field)


def newton(load, state, ratio, strength):
    scale = 0.5 * jnp.exp(ratio * state)
    product = strength * scale
    velocity = load / (product + damping)
    for _ in range(NEWTON):
        scaled = scale * velocity
        magnitude = jnp.abs(scaled)
        root = jnp.sqrt(magnitude * magnitude + 1.0)
        positive = jnp.log(magnitude + root)
        arc = jnp.where(scaled < 0.0, -positive, positive)
        residual = strength * arc + damping * velocity - load
        velocity = velocity - residual / (product / root + damping)
    return velocity


def evolved(state, speed_of):
    return state + time_step * (jnp.exp(-state) - jnp.sqrt(speed_of * speed_of + creep_square))


def scatter_sum(parts):
    lags = len(parts)
    total = parts[0]
    for d in range(1, lags):
        route = [(i, (i + d) % lags) for i in range(lags)]
        total = total + lax.ppermute(parts[d], "lag", route).astype(jnp.float32)
    return total


def settle_friction(shear_load, state, ratio, strength):
    velocity = newton(shear_load, state, ratio, strength)
    return velocity.astype(jnp.bfloat16), evolved(state, velocity)


def tree_to_first(value, lags, least):
    received, stride = [], 1
    while stride < lags:
        route = [(i + stride, i) for i in range(0, lags - stride, 2 * stride) if i + stride >= least]
        arrived = lax.ppermute(value, "lag", route)
        if route[0][1] == 0:
            received.append(arrived)
        stride *= 2
        if stride < lags:
            total = value.astype(jnp.float32) + arrived.astype(jnp.float32)
            value = lax.optimization_barrier(total.astype(jnp.bfloat16))
    return received


def shards(kernel_tiles, shell_index, cone_blocks, history, prestress, log_state, fric_a, fric_b, normal_stress):
    lags = lax.axis_size("lag")
    me = lax.axis_index("lag")
    every, rest = list(range(lags)), list(range(1, lags))
    local = (shell_index, cone_blocks, kernel_tiles)
    field = history[0]
    rows = prestress.shape[2]

    def window_of(own, planes):
        below, above = exchange(own, planes)
        return below, own, above

    def block_load(high, *received):
        load = high
        for part in received:
            load = load + part.astype(jnp.float32)
        return load

    below, own, above = window_of(field, every)
    packed = pack(log_state, fric_a, fric_b, normal_stress, kernel_tiles, field)
    packed = [packed] + [lax.ppermute(packed, "lag", [(d, 0)]) for d in rest]
    once = lax.ppermute(field, "lag", [(i, i + 1) for i in every[:-1]])
    traction = scatter_sum(product_by_rows(*local, below, own, above, lags))
    coef_a, coef_b, sigma = (c[0, 0][:, None] for c in (fric_a, fric_b, normal_stress))
    row_pair = (coef_b / coef_a, sigma * coef_a)
    rates, _ = settle_friction(prestress[0, 0] + traction, log_state[0, 0], *row_pair)
    first = lax.all_gather(rates, "lag", axis=0, tiled=True)
    packed, first = lax.optimization_barrier((packed, first))
    state = jnp.concatenate([g[:rows] for g in packed], 0)
    ratio, strength = (jnp.concatenate([g[rows + k, :rows] for g in packed])[:, None] for k in range(2))
    state = evolved(state, first.astype(jnp.float32))

    kinds = [jnp.float32, jnp.bfloat16]
    (low,) = block_product(*local, window_of(once, rest), prestress, rest, kinds[1:])
    base_1 = tree_to_first(low, lags, 1)
    twice = lax.ppermute(once, "lag", [(i, i + 1) for i in rest[:-1]])
    (low,) = block_product(*local, window_of(twice, rest[1:]), prestress, rest[1:], kinds[1:])
    base_2 = tree_to_first(low, lags, 2)

    window = window_of(first, [0, 1])
    high, low = block_product(*local, window, prestress, [0, 1], kinds)
    base_2 = base_2 + [lax.ppermute(low, "lag", [(1, 0)])]
    second, state = settle_friction(block_load(high, *base_1), state, ratio, strength)
    window = window_of(second, [0])
    (high,) = block_product(*local, window, prestress, [0], kinds[:1])
    third, state = settle_friction(block_load(high, *base_2), state, ratio, strength)

    source = jnp.where(me == 0, second, twice)
    moved = lax.ppermute(source, "lag", [(0, 1)] + [(i, i + 1) for i in every[2:-1]])
    last = jnp.where(me == 0, third, jnp.where(me == 2, first, moved))
    below, own, above = window_of(last, every)
    mine = state[:rows]
    for d in rest:
        piece = lax.ppermute(state[d * rows : (d + 1) * rows], "lag", [(0, d)])
        mine = jnp.where(me == d, piece, mine)
    traction = scatter_sum(product_by_rows(*local, below, own, above, lags))
    rates, state = settle_friction(prestress[0, 0] + traction, mine, *row_pair)
    return rates[None, None], state[None, None]


def solution(mesh):
    in_specs = (
        P("lag", "elem", None),
        P("lag", "elem", None),
        P("lag"),
        P("lag", "elem", None),
        P("elem", "lag", None, None),
        P("elem", "lag", None, None),
        P("elem", "lag", None),
        P("elem", "lag", None),
        P("elem", "lag", None),
    )
    out_specs = (P("elem", "lag", None, None), P("elem", "lag", None, None))
    return jax.shard_map(shards, mesh=mesh, in_specs=in_specs, out_specs=out_specs, check_vma=False)
```

```python
import functools

import jax
import jax.numpy as jnp
from jax import lax
from jax.experimental import pallas as pl
from jax.experimental.pallas import tpu as pltpu
from jax.sharding import PartitionSpec as P


NEWTON = 3

damping = 0.5
time_step = 0.25
creep_square = 0.01

ANY = pl.BlockSpec(memory_space=pl.ANY)
VMEM = pl.BlockSpec(memory_space=pltpu.VMEM)
PARAMS = pltpu.CompilerParams(vmem_limit_bytes=32 * 1024 * 1024)


def exchange(value, planes):
    count = lax.axis_size("elem")
    up = [(i * count + j, i * count + j + 1) for i in planes for j in range(count - 1)]
    down = [(j, i) for i, j in up]
    axes = ("lag", "elem")
    return lax.ppermute(value, axes, up), lax.ppermute(value, axes, down)


def fetch(picks, live, below, own, above, sources, sems):
    slots = sems.shape[0]
    block = sources.shape[0] // slots
    per = own.shape[0] // block
    alive = live[0]
    for k in range(slots):
        spot = sources.at[pl.ds(k * block, block)]
        pick = picks[0, 0, k]
        start = pl.multiple_of(lax.rem(pick, per) * block, block)
        for which, ref in enumerate((below, own, above)):

            @pl.when((k < alive) & (lax.div(pick, per) == which))
            def _():
                pltpu.make_async_copy(ref.at[pl.ds(start, block)], spot, sems.at[k]).start()

    for k in range(slots):
        spot = sources.at[pl.ds(k * block, block)]

        @pl.when(k >= alive)
        def _():
            spot[...] = jnp.zeros(spot.shape, spot.dtype)

        @pl.when(k < alive)
        def _():
            pltpu.make_async_copy(own.at[pl.ds(0, block)], spot, sems.at[k]).wait()


def rows_kernel(lags, rows, picks, live, tile, below, own, above, *refs):
    outs, sources, sems = refs[:lags], refs[lags], refs[lags + 1]
    me = lax.axis_index("lag")
    fetch(picks, live, below, own, above, sources, sems)
    for d in range(lags):
        first = pl.multiple_of(lax.rem(me + d, lags) * rows, rows)
        part = jnp.dot(tile[0, pl.ds(first, rows), :], sources[...], preferred_element_type=jnp.float32)
        outs[d][...] = part.astype(outs[d].dtype)


def product_by_rows(picks, live, tile, below, own, above, lags):
    rows, cols = own.shape[0] // lags, own.shape[1]
    kinds = [jnp.float32] + [jnp.bfloat16] * (lags - 1)
    return pl.pallas_call(
        functools.partial(rows_kernel, lags, rows),
        grid_spec=pltpu.PrefetchScalarGridSpec(
            num_scalar_prefetch=2,
            grid=(1,),
            in_specs=[VMEM] + [ANY] * 3,
            out_specs=[VMEM] * lags,
            scratch_shapes=[pltpu.VMEM((tile.shape[2], cols), own.dtype), pltpu.SemaphoreType.DMA((picks.shape[2],))],
        ),
        out_shape=[jax.ShapeDtypeStruct((rows, cols), kind) for kind in kinds],
        compiler_params=PARAMS,
        cost_estimate=pl.CostEstimate(
            flops=2 * tile.size * cols, bytes_accessed=2 * (tile.size + 4 * own.size), transcendentals=0
        ),
        name="product_by_rows",
    )(picks, live, tile, below, own, above)


def block_kernel(chunks, planes, high_too, picks, live, tile, below, own, above, stress, *refs):
    outs, sources, sems = refs[:-2], refs[-2], refs[-1]
    me = lax.axis_index("lag")
    rows, height = own.shape[0] // chunks, stress.shape[2]
    mine = pl.ds(pl.multiple_of(me * height, height), height)

    def write(out):
        for d in range(chunks):
            spot = pl.ds(d * rows, rows)
            part = jnp.dot(tile[0, spot, :], sources[...], preferred_element_type=jnp.float32)
            out[spot, :] = part.astype(out.dtype)
        part = jnp.dot(tile[0, mine, :], sources[...], preferred_element_type=jnp.float32)
        out[mine, :] = (part + stress[0, 0]).astype(out.dtype)

    @pl.when((me >= planes[0]) & (me <= planes[-1]))
    def _():
        fetch(picks, live, below, own, above, sources, sems)
        if high_too:

            @pl.when(me == 0)
            def _():
                write(outs[0])

            @pl.when(me > 0)
            def _():
                write(outs[1])

        else:
            write(outs[0])


def block_product(picks, live, tile, window, stress, planes, kinds):
    below, own, above = window
    chunks = max(1, tile.shape[1] // 256)
    return pl.pallas_call(
        functools.partial(block_kernel, chunks, (planes[0], planes[-1]), len(kinds) > 1),
        grid_spec=pltpu.PrefetchScalarGridSpec(
            num_scalar_prefetch=2,
            grid=(1,),
            in_specs=[VMEM] + [ANY] * 3 + [VMEM],
            out_specs=[VMEM] * len(kinds),
            scratch_shapes=[
                pltpu.VMEM((tile.shape[2], own.shape[1]), own.dtype),
                pltpu.SemaphoreType.DMA((picks.shape[2],)),
            ],
        ),
        out_shape=[jax.ShapeDtypeStruct(own.shape, kind) for kind in kinds],
        compiler_params=PARAMS,
        cost_estimate=pl.CostEstimate(
            flops=2 * tile.size * own.shape[1], bytes_accessed=2 * (tile.size + 4 * own.size), transcendentals=0
        ),
        name="block_product",
    )(picks, live, tile, below, own, above, stress)


def pack_kernel(state, coef_a, coef_b, sigma, out):
    rows = state.shape[2]
    out[pl.ds(0, rows), :] = state[0, 0]
    out[pl.ds(rows, 8), :] = jnp.zeros((8, out.shape[1]), out.dtype)
    out[pl.ds(rows, 1), pl.ds(0, rows)] = coef_b[0] / coef_a[0]
    out[pl.ds(rows + 1, 1), pl.ds(0, rows)] = sigma[0] * coef_a[0]


def pack(state, coef_a, coef_b, sigma):
    return pl.pallas_call(
        pack_kernel,
        in_specs=[VMEM] * 4,
        out_specs=VMEM,
        out_shape=jax.ShapeDtypeStruct((state.shape[2] + 8, state.shape[3]), jnp.float32),
        compiler_params=PARAMS,
        name="pack",
    )(state, coef_a, coef_b, sigma)


def touch(*arrays):
    pl.pallas_call(
        lambda *refs: refs[-1].__setitem__(Ellipsis, jnp.zeros(refs[-1].shape, refs[-1].dtype)),
        in_specs=[ANY] * len(arrays),
        out_specs=VMEM,
        out_shape=jax.ShapeDtypeStruct((8, 128), jnp.float32),
        compiler_params=pltpu.CompilerParams(vmem_limit_bytes=32 * 1024 * 1024, has_side_effects=True),
        name="touch",
    )(*arrays)


def newton(load, state, ratio, strength):
    scale = 0.5 * jnp.exp(ratio * state)
    product = strength * scale
    velocity = load / (product + damping)
    for _ in range(NEWTON):
        scaled = scale * velocity
        magnitude = jnp.abs(scaled)
        root = jnp.sqrt(magnitude * magnitude + 1.0)
        positive = jnp.log(magnitude + root)
        arc = jnp.where(scaled < 0.0, -positive, positive)
        residual = strength * arc + damping * velocity - load
        velocity = velocity - residual / (product / root + damping)
    return velocity


def evolved(state, speed_of):
    return state + time_step * (jnp.exp(-state) - jnp.sqrt(speed_of * speed_of + creep_square))


def scatter_sum(parts):
    lags = len(parts)
    total = parts[0]
    for d in range(1, lags):
        route = [(i, (i + d) % lags) for i in range(lags)]
        total = total + lax.ppermute(parts[d], "lag", route).astype(jnp.float32)
    return total


def settle_friction(shear_load, state, ratio, strength):
    velocity = newton(shear_load, state, ratio, strength)
    return velocity.astype(jnp.bfloat16), evolved(state, velocity)


def tree_to_first(value, lags, least):
    received, stride = [], 1
    while stride < lags:
        route = [(i + stride, i) for i in range(0, lags - stride, 2 * stride) if i + stride >= least]
        arrived = lax.ppermute(value, "lag", route)
        if route[0][1] == 0:
            received.append(arrived)
        stride *= 2
        if stride < lags:
            total = value.astype(jnp.float32) + arrived.astype(jnp.float32)
            value = lax.optimization_barrier(total.astype(jnp.bfloat16))
    return received


def shards(kernel_tiles, shell_index, cone_blocks, history, prestress, log_state, fric_a, fric_b, normal_stress):
    lags = lax.axis_size("lag")
    me = lax.axis_index("lag")
    every, rest = list(range(lags)), list(range(1, lags))
    local = (shell_index, cone_blocks, kernel_tiles)
    field = history[0]
    rows = prestress.shape[2]

    def window_of(own, planes):
        below, above = exchange(own, planes)
        return below, own, above

    def block_load(high, *received):
        load = high
        for part in received:
            load = load + part.astype(jnp.float32)
        return load

    below, own, above = window_of(field, every)
    packed = pack(log_state, fric_a, fric_b, normal_stress)
    packed = [packed] + [lax.ppermute(packed, "lag", [(d, 0)]) for d in rest]
    once = lax.ppermute(field, "lag", [(i, i + 1) for i in every[:-1]])
    touch(kernel_tiles, field)
    traction = scatter_sum(product_by_rows(*local, below, own, above, lags))
    coef_a, coef_b, sigma = (c[0, 0][:, None] for c in (fric_a, fric_b, normal_stress))
    row_pair = (coef_b / coef_a, sigma * coef_a)
    rates, _ = settle_friction(prestress[0, 0] + traction, log_state[0, 0], *row_pair)
    first = lax.all_gather(rates, "lag", axis=0, tiled=True)
    kinds = [jnp.float32, jnp.bfloat16]
    (low,) = block_product(*local, window_of(once, rest), prestress, rest, kinds[1:])
    base_1 = tree_to_first(low, lags, 1)
    twice = lax.ppermute(once, "lag", [(i, i + 1) for i in rest[:-1]])
    window_2 = window_of(twice, rest[1:])
    packed, _ = lax.optimization_barrier((packed, window_2[0]))
    state = jnp.concatenate([g[:rows] for g in packed], 0)
    ratio, strength = (jnp.concatenate([g[rows + k, :rows] for g in packed])[:, None] for k in range(2))
    state = evolved(state, first.astype(jnp.float32))
    (low,) = block_product(*local, window_2, prestress, rest[1:], kinds[1:])
    base_2 = tree_to_first(low, lags, 2)

    window = window_of(first, [0, 1])
    high, low = block_product(*local, window, prestress, [0, 1], kinds)
    base_2 = base_2 + [lax.ppermute(low, "lag", [(1, 0)])]
    second, state = settle_friction(block_load(high, *base_1), state, ratio, strength)
    window = window_of(second, [0])
    (high,) = block_product(*local, window, prestress, [0], kinds[:1])
    third, state = settle_friction(block_load(high, *base_2), state, ratio, strength)

    source = jnp.where(me == 0, second, twice)
    moved = lax.ppermute(source, "lag", [(0, 1)] + [(i, i + 1) for i in every[2:-1]])
    last = jnp.where(me == 0, third, jnp.where(me == 2, first, moved))
    below, own, above = window_of(last, every)
    mine = state[:rows]
    for d in rest:
        piece = lax.ppermute(state[d * rows : (d + 1) * rows], "lag", [(0, d)])
        mine = jnp.where(me == d, piece, mine)
    traction = scatter_sum(product_by_rows(*local, below, own, above, lags))
    rates, state = settle_friction(prestress[0, 0] + traction, mine, *row_pair)
    return rates[None, None], state[None, None]


def solution(mesh):
    in_specs = (
        P("lag", "elem", None),
        P("lag", "elem", None),
        P("lag"),
        P("lag", "elem", None),
        P("elem", "lag", None, None),
        P("elem", "lag", None, None),
        P("elem", "lag", None),
        P("elem", "lag", None),
        P("elem", "lag", None),
    )
    out_specs = (P("elem", "lag", None, None), P("elem", "lag", None, None))
    return jax.shard_map(shards, mesh=mesh, in_specs=in_specs, out_specs=out_specs, check_vma=False)
```

```python
import functools

import jax
import jax.numpy as jnp
from jax import lax
from jax.experimental import pallas as pl
from jax.experimental.pallas import tpu as pltpu
from jax.sharding import PartitionSpec as P


NEWTON = 3

damping = 0.5
time_step = 0.25
creep_square = 0.01

ANY = pl.BlockSpec(memory_space=pl.ANY)
VMEM = pl.BlockSpec(memory_space=pltpu.VMEM)
PARAMS = pltpu.CompilerParams(vmem_limit_bytes=32 * 1024 * 1024)


def exchange(value, planes):
    count = lax.axis_size("elem")
    up = [(i * count + j, i * count + j + 1) for i in planes for j in range(count - 1)]
    down = [(j, i) for i, j in up]
    axes = ("lag", "elem")
    return lax.ppermute(value, axes, up), lax.ppermute(value, axes, down)


def fetch(picks, live, below, own, above, sources, sems):
    slots = sems.shape[0]
    block = sources.shape[0] // slots
    per = own.shape[0] // block
    alive = live[0]
    for k in range(slots):
        spot = sources.at[pl.ds(k * block, block)]
        pick = picks[0, 0, k]
        start = pl.multiple_of(lax.rem(pick, per) * block, block)
        for which, ref in enumerate((below, own, above)):

            @pl.when((k < alive) & (lax.div(pick, per) == which))
            def _():
                pltpu.make_async_copy(ref.at[pl.ds(start, block)], spot, sems.at[k]).start()

    for k in range(slots):
        spot = sources.at[pl.ds(k * block, block)]

        @pl.when(k >= alive)
        def _():
            spot[...] = jnp.zeros(spot.shape, spot.dtype)

        @pl.when(k < alive)
        def _():
            pltpu.make_async_copy(own.at[pl.ds(0, block)], spot, sems.at[k]).wait()


def rows_kernel(lags, rows, picks, live, tile, below, own, above, *refs):
    outs, sources, sems = refs[:lags], refs[lags], refs[lags + 1]
    me = lax.axis_index("lag")
    fetch(picks, live, below, own, above, sources, sems)
    for d in range(lags):
        first = pl.multiple_of(lax.rem(me + d, lags) * rows, rows)
        part = jnp.dot(tile[0, pl.ds(first, rows), :], sources[...], preferred_element_type=jnp.float32)
        outs[d][...] = part.astype(outs[d].dtype)


def product_by_rows(picks, live, tile, below, own, above, lags):
    rows, cols = own.shape[0] // lags, own.shape[1]
    kinds = [jnp.float32] + [jnp.bfloat16] * (lags - 1)
    return pl.pallas_call(
        functools.partial(rows_kernel, lags, rows),
        grid_spec=pltpu.PrefetchScalarGridSpec(
            num_scalar_prefetch=2,
            grid=(1,),
            in_specs=[VMEM] + [ANY] * 3,
            out_specs=[VMEM] * lags,
            scratch_shapes=[pltpu.VMEM((tile.shape[2], cols), own.dtype), pltpu.SemaphoreType.DMA((picks.shape[2],))],
        ),
        out_shape=[jax.ShapeDtypeStruct((rows, cols), kind) for kind in kinds],
        compiler_params=PARAMS,
        cost_estimate=pl.CostEstimate(
            flops=2 * tile.size * cols, bytes_accessed=2 * (tile.size + 4 * own.size), transcendentals=0
        ),
        name="product_by_rows",
    )(picks, live, tile, below, own, above)


def block_kernel(chunks, planes, high_too, picks, live, tile, below, own, above, stress, *refs):
    outs, sources, sems = refs[:-2], refs[-2], refs[-1]
    me = lax.axis_index("lag")
    rows, height = own.shape[0] // chunks, stress.shape[2]
    mine = pl.ds(pl.multiple_of(me * height, height), height)

    def write(out):
        for d in range(chunks):
            spot = pl.ds(d * rows, rows)
            part = jnp.dot(tile[0, spot, :], sources[...], preferred_element_type=jnp.float32)
            out[spot, :] = part.astype(out.dtype)
        part = jnp.dot(tile[0, mine, :], sources[...], preferred_element_type=jnp.float32)
        out[mine, :] = (part + stress[0, 0]).astype(out.dtype)

    @pl.when((me >= planes[0]) & (me <= planes[-1]))
    def _():
        fetch(picks, live, below, own, above, sources, sems)
        if high_too:

            @pl.when(me == 0)
            def _():
                write(outs[0])

            @pl.when(me > 0)
            def _():
                write(outs[1])

        else:
            write(outs[0])


def block_product(picks, live, tile, window, stress, planes, kinds):
    below, own, above = window
    chunks = max(1, tile.shape[1] // 256)
    return pl.pallas_call(
        functools.partial(block_kernel, chunks, (planes[0], planes[-1]), len(kinds) > 1),
        grid_spec=pltpu.PrefetchScalarGridSpec(
            num_scalar_prefetch=2,
            grid=(1,),
            in_specs=[VMEM] + [ANY] * 3 + [VMEM],
            out_specs=[VMEM] * len(kinds),
            scratch_shapes=[
                pltpu.VMEM((tile.shape[2], own.shape[1]), own.dtype),
                pltpu.SemaphoreType.DMA((picks.shape[2],)),
            ],
        ),
        out_shape=[jax.ShapeDtypeStruct(own.shape, kind) for kind in kinds],
        compiler_params=PARAMS,
        cost_estimate=pl.CostEstimate(
            flops=2 * tile.size * own.shape[1], bytes_accessed=2 * (tile.size + 4 * own.size), transcendentals=0
        ),
        name="block_product",
    )(picks, live, tile, below, own, above, stress)


def pack_kernel(state, coef_a, coef_b, sigma, out):
    rows = state.shape[2]
    out[pl.ds(0, rows), :] = state[0, 0]
    out[pl.ds(rows, 8), :] = jnp.zeros((8, out.shape[1]), out.dtype)
    out[pl.ds(rows, 1), pl.ds(0, rows)] = coef_b[0] / coef_a[0]
    out[pl.ds(rows + 1, 1), pl.ds(0, rows)] = sigma[0] * coef_a[0]


def pack(state, coef_a, coef_b, sigma):
    return pl.pallas_call(
        pack_kernel,
        in_specs=[VMEM] * 4,
        out_specs=VMEM,
        out_shape=jax.ShapeDtypeStruct((state.shape[2] + 8, state.shape[3]), jnp.float32),
        compiler_params=PARAMS,
        name="pack",
    )(state, coef_a, coef_b, sigma)


def unpack_kernel(lags, *refs):
    packed, state, columns = refs[:lags], refs[lags], refs[lags + 1]
    rows = state.shape[0] // lags

    @pl.when(lax.axis_index("lag") == 0)
    def _():
        for d, ref in enumerate(packed):
            spot = pl.ds(d * rows, rows)
            state[spot, :] = ref[pl.ds(0, rows), :]
            columns[spot, :] = jnp.transpose(ref[pl.ds(rows, 8), :])[:rows]


def unpack(packed):
    lags, (height, cols) = len(packed), packed[0].shape
    rows = (height - 8) * lags
    return pl.pallas_call(
        functools.partial(unpack_kernel, lags),
        in_specs=[VMEM] * lags,
        out_specs=[VMEM] * 2,
        out_shape=[jax.ShapeDtypeStruct((rows, cols), jnp.float32), jax.ShapeDtypeStruct((rows, 8), jnp.float32)],
        compiler_params=PARAMS,
        name="unpack",
    )(*packed)


def touch(*arrays):
    pl.pallas_call(
        lambda *refs: refs[-1].__setitem__(Ellipsis, jnp.zeros(refs[-1].shape, refs[-1].dtype)),
        in_specs=[ANY] * len(arrays),
        out_specs=VMEM,
        out_shape=jax.ShapeDtypeStruct((8, 128), jnp.float32),
        compiler_params=pltpu.CompilerParams(vmem_limit_bytes=32 * 1024 * 1024, has_side_effects=True),
        name="touch",
    )(*arrays)


def newton(load, state, ratio, strength):
    scale = 0.5 * jnp.exp(ratio * state)
    product = strength * scale
    velocity = load / (product + damping)
    for _ in range(NEWTON):
        scaled = scale * velocity
        magnitude = jnp.abs(scaled)
        root = jnp.sqrt(magnitude * magnitude + 1.0)
        positive = jnp.log(magnitude + root)
        arc = jnp.where(scaled < 0.0, -positive, positive)
        residual = strength * arc + damping * velocity - load
        velocity = velocity - residual / (product / root + damping)
    return velocity


def evolved(state, speed_of):
    return state + time_step * (jnp.exp(-state) - jnp.sqrt(speed_of * speed_of + creep_square))


def scatter_sum(parts):
    lags = len(parts)
    total = parts[0]
    for d in range(1, lags):
        route = [(i, (i + d) % lags) for i in range(lags)]
        total = total + lax.ppermute(parts[d], "lag", route).astype(jnp.float32)
    return total


def settle_friction(shear_load, state, ratio, strength):
    velocity = newton(shear_load, state, ratio, strength)
    return velocity.astype(jnp.bfloat16), evolved(state, velocity)


def tree_to_first(value, lags, least):
    received, stride = [], 1
    while stride < lags:
        route = [(i + stride, i) for i in range(0, lags - stride, 2 * stride) if i + stride >= least]
        arrived = lax.ppermute(value, "lag", route)
        if route[0][1] == 0:
            received.append(arrived)
        stride *= 2
        if stride < lags:
            total = value.astype(jnp.float32) + arrived.astype(jnp.float32)
            value = lax.optimization_barrier(total.astype(jnp.bfloat16))
    return received


def shards(kernel_tiles, shell_index, cone_blocks, history, prestress, log_state, fric_a, fric_b, normal_stress):
    lags = lax.axis_size("lag")
    me = lax.axis_index("lag")
    every, rest = list(range(lags)), list(range(1, lags))
    local = (shell_index, cone_blocks, kernel_tiles)
    field = history[0]
    rows = prestress.shape[2]

    def window_of(own, planes):
        below, above = exchange(own, planes)
        return below, own, above

    def block_load(high, *received):
        load = high
        for part in received:
            load = load + part.astype(jnp.float32)
        return load

    below, own, above = window_of(field, every)
    packed = pack(log_state, fric_a, fric_b, normal_stress)
    packed = [packed] + [lax.ppermute(packed, "lag", [(d, 0)]) for d in rest]
    once = lax.ppermute(field, "lag", [(i, i + 1) for i in every[:-1]])
    touch(kernel_tiles, field)
    traction = scatter_sum(product_by_rows(*local, below, own, above, lags))
    coef_a, coef_b, sigma = (c[0, 0][:, None] for c in (fric_a, fric_b, normal_stress))
    row_pair = (coef_b / coef_a, sigma * coef_a)
    rates, _ = settle_friction(prestress[0, 0] + traction, log_state[0, 0], *row_pair)
    first = lax.all_gather(rates, "lag", axis=0, tiled=True)
    kinds = [jnp.float32, jnp.bfloat16]
    (low,) = block_product(*local, window_of(once, rest), prestress, rest, kinds[1:])
    base_1 = tree_to_first(low, lags, 1)
    twice = lax.ppermute(once, "lag", [(i, i + 1) for i in rest[:-1]])
    window_2 = window_of(twice, rest[1:])
    state, columns = unpack(packed)
    (low,) = block_product(*local, window_2, prestress, rest[1:], kinds[1:])
    base_2 = tree_to_first(low, lags, 2)

    window = window_of(first, [0, 1])
    high, low = block_product(*local, window, prestress, [0, 1], kinds)
    base_2 = base_2 + [lax.ppermute(low, "lag", [(1, 0)])]

    def on_first(step, *values):
        like = (jax.ShapeDtypeStruct(field.shape, jnp.bfloat16), jax.ShapeDtypeStruct(field.shape, jnp.float32))
        return lax.cond(me == 0, step, lambda *_: tuple(jnp.zeros(x.shape, x.dtype) for x in like), *values)

    def second_step(high, start, first, columns, *received):
        begun = evolved(start, first.astype(jnp.float32))
        return settle_friction(block_load(high, *received), begun, columns[:, 0:1], columns[:, 1:2])

    def third_step(high, start, columns, *received):
        return settle_friction(block_load(high, *received), start, columns[:, 0:1], columns[:, 1:2])

    second, state = on_first(second_step, high, state, first, columns, *base_1)
    window = window_of(second, [0])
    (high,) = block_product(*local, window, prestress, [0], kinds[:1])
    third, state = on_first(third_step, high, state, columns, *base_2)

    source = jnp.where(me == 0, second, twice)
    moved = lax.ppermute(source, "lag", [(0, 1)] + [(i, i + 1) for i in every[2:-1]])
    last = jnp.where(me == 0, third, jnp.where(me == 2, first, moved))
    below, own, above = window_of(last, every)
    mine = state[:rows]
    for d in rest:
        piece = lax.ppermute(state[d * rows : (d + 1) * rows], "lag", [(0, d)])
        mine = jnp.where(me == d, piece, mine)
    traction = scatter_sum(product_by_rows(*local, below, own, above, lags))
    rates, state = settle_friction(prestress[0, 0] + traction, mine, *row_pair)
    return rates[None, None], state[None, None]


def solution(mesh):
    in_specs = (
        P("lag", "elem", None),
        P("lag", "elem", None),
        P("lag"),
        P("lag", "elem", None),
        P("elem", "lag", None, None),
        P("elem", "lag", None, None),
        P("elem", "lag", None),
        P("elem", "lag", None),
        P("elem", "lag", None),
    )
    out_specs = (P("elem", "lag", None, None), P("elem", "lag", None, None))
    return jax.shard_map(shards, mesh=mesh, in_specs=in_specs, out_specs=out_specs, check_vma=False)
```

```python
import functools

import jax
import jax.numpy as jnp
from jax import lax
from jax.experimental import pallas as pl
from jax.experimental.pallas import tpu as pltpu
from jax.sharding import PartitionSpec as P


NEWTON = 3

damping = 0.5
time_step = 0.25
creep_square = 0.01

ANY = pl.BlockSpec(memory_space=pl.ANY)
VMEM = pl.BlockSpec(memory_space=pltpu.VMEM)
PARAMS = pltpu.CompilerParams(vmem_limit_bytes=32 * 1024 * 1024)


def exchange(value, planes):
    count = lax.axis_size("elem")
    up = [(i * count + j, i * count + j + 1) for i in planes for j in range(count - 1)]
    down = [(j, i) for i, j in up]
    axes = ("lag", "elem")
    return lax.ppermute(value, axes, up), lax.ppermute(value, axes, down)


def fetch(picks, live, below, own, above, sources, sems):
    slots = sems.shape[0]
    block = sources.shape[0] // slots
    per = own.shape[0] // block
    alive = live[0]
    for k in range(slots):
        spot = sources.at[pl.ds(k * block, block)]
        pick = picks[0, 0, k]
        start = pl.multiple_of(lax.rem(pick, per) * block, block)
        for which, ref in enumerate((below, own, above)):

            @pl.when((k < alive) & (lax.div(pick, per) == which))
            def _():
                pltpu.make_async_copy(ref.at[pl.ds(start, block)], spot, sems.at[k]).start()

    for k in range(slots):
        spot = sources.at[pl.ds(k * block, block)]

        @pl.when(k >= alive)
        def _():
            spot[...] = jnp.zeros(spot.shape, spot.dtype)

        @pl.when(k < alive)
        def _():
            pltpu.make_async_copy(own.at[pl.ds(0, block)], spot, sems.at[k]).wait()


def rows_kernel(lags, rows, picks, live, tile, below, own, above, *refs):
    outs, sources, sems = refs[:lags], refs[lags], refs[lags + 1]
    me = lax.axis_index("lag")
    fetch(picks, live, below, own, above, sources, sems)
    for d in range(lags):
        first = pl.multiple_of(lax.rem(me + d, lags) * rows, rows)
        part = jnp.dot(tile[0, pl.ds(first, rows), :], sources[...], preferred_element_type=jnp.float32)
        outs[d][...] = part.astype(outs[d].dtype)


def product_by_rows(picks, live, tile, below, own, above, lags):
    rows, cols = own.shape[0] // lags, own.shape[1]
    kinds = [jnp.float32] + [jnp.bfloat16] * (lags - 1)
    return pl.pallas_call(
        functools.partial(rows_kernel, lags, rows),
        grid_spec=pltpu.PrefetchScalarGridSpec(
            num_scalar_prefetch=2,
            grid=(1,),
            in_specs=[VMEM] + [ANY] * 3,
            out_specs=[VMEM] * lags,
            scratch_shapes=[pltpu.VMEM((tile.shape[2], cols), own.dtype), pltpu.SemaphoreType.DMA((picks.shape[2],))],
        ),
        out_shape=[jax.ShapeDtypeStruct((rows, cols), kind) for kind in kinds],
        compiler_params=PARAMS,
        cost_estimate=pl.CostEstimate(
            flops=2 * tile.size * cols, bytes_accessed=2 * (tile.size + 4 * own.size), transcendentals=0
        ),
        name="product_by_rows",
    )(picks, live, tile, below, own, above)


def block_kernel(chunks, planes, high_too, picks, live, tile, below, own, above, stress, *refs):
    outs, sources, sems = refs[:-2], refs[-2], refs[-1]
    me = lax.axis_index("lag")
    rows, height = own.shape[0] // chunks, stress.shape[2]
    mine = pl.ds(pl.multiple_of(me * height, height), height)

    def write(out):
        for d in range(chunks):
            spot = pl.ds(d * rows, rows)
            part = jnp.dot(tile[0, spot, :], sources[...], preferred_element_type=jnp.float32)
            out[spot, :] = part.astype(out.dtype)
        part = jnp.dot(tile[0, mine, :], sources[...], preferred_element_type=jnp.float32)
        out[mine, :] = (part + stress[0, 0]).astype(out.dtype)

    @pl.when((me >= planes[0]) & (me <= planes[-1]))
    def _():
        fetch(picks, live, below, own, above, sources, sems)
        if high_too:

            @pl.when(me == 0)
            def _():
                write(outs[0])

            @pl.when(me > 0)
            def _():
                write(outs[1])

        else:
            write(outs[0])


def block_product(picks, live, tile, window, stress, planes, kinds):
    below, own, above = window
    chunks = max(1, tile.shape[1] // 256)
    return pl.pallas_call(
        functools.partial(block_kernel, chunks, (planes[0], planes[-1]), len(kinds) > 1),
        grid_spec=pltpu.PrefetchScalarGridSpec(
            num_scalar_prefetch=2,
            grid=(1,),
            in_specs=[VMEM] + [ANY] * 3 + [VMEM],
            out_specs=[VMEM] * len(kinds),
            scratch_shapes=[
                pltpu.VMEM((tile.shape[2], own.shape[1]), own.dtype),
                pltpu.SemaphoreType.DMA((picks.shape[2],)),
            ],
        ),
        out_shape=[jax.ShapeDtypeStruct(own.shape, kind) for kind in kinds],
        compiler_params=PARAMS,
        cost_estimate=pl.CostEstimate(
            flops=2 * tile.size * own.shape[1], bytes_accessed=2 * (tile.size + 4 * own.size), transcendentals=0
        ),
        name="block_product",
    )(picks, live, tile, below, own, above, stress)


def pack_kernel(state, coef_a, coef_b, sigma, out):
    rows = state.shape[2]
    out[pl.ds(0, rows), :] = state[0, 0]
    out[pl.ds(rows, 8), :] = jnp.zeros((8, out.shape[1]), out.dtype)
    out[pl.ds(rows, 1), pl.ds(0, rows)] = coef_b[0] / coef_a[0]
    out[pl.ds(rows + 1, 1), pl.ds(0, rows)] = sigma[0] * coef_a[0]


def pack(state, coef_a, coef_b, sigma):
    return pl.pallas_call(
        pack_kernel,
        in_specs=[VMEM] * 4,
        out_specs=VMEM,
        out_shape=jax.ShapeDtypeStruct((state.shape[2] + 8, state.shape[3]), jnp.float32),
        compiler_params=PARAMS,
        name="pack",
    )(state, coef_a, coef_b, sigma)


def unpack_kernel(lags, *refs):
    packed, state, columns = refs[:lags], refs[lags], refs[lags + 1]
    rows = state.shape[0] // lags

    @pl.when(lax.axis_index("lag") == 0)
    def _():
        for d, ref in enumerate(packed):
            spot = pl.ds(d * rows, rows)
            state[spot, :] = ref[pl.ds(0, rows), :]
            columns[spot, :] = jnp.transpose(ref[pl.ds(rows, 8), :])[:rows]


def unpack(packed):
    lags, (height, cols) = len(packed), packed[0].shape
    rows = (height - 8) * lags
    return pl.pallas_call(
        functools.partial(unpack_kernel, lags),
        in_specs=[VMEM] * lags,
        out_specs=[VMEM] * 2,
        out_shape=[jax.ShapeDtypeStruct((rows, cols), jnp.float32), jax.ShapeDtypeStruct((rows, 8), jnp.float32)],
        compiler_params=PARAMS,
        name="unpack",
    )(*packed)


def assemble_kernel(*refs):
    parts, out = refs[:-1], refs[-1]
    me, lags = lax.axis_index("lag"), len(parts)
    rows = parts[0].shape[0]
    for d, part in enumerate(parts):
        spot = pl.multiple_of(lax.rem(me + lags - d, lags) * rows, rows)
        out[pl.ds(spot, rows), :] = part[...]


def assemble(parts):
    rows, cols = parts[0].shape
    return pl.pallas_call(
        assemble_kernel,
        in_specs=[VMEM] * len(parts),
        out_specs=VMEM,
        out_shape=jax.ShapeDtypeStruct((rows * len(parts), cols), parts[0].dtype),
        compiler_params=PARAMS,
        name="assemble",
    )(*parts)


def touch(*arrays):
    pl.pallas_call(
        lambda *refs: refs[-1].__setitem__(Ellipsis, jnp.zeros(refs[-1].shape, refs[-1].dtype)),
        in_specs=[ANY] * len(arrays),
        out_specs=VMEM,
        out_shape=jax.ShapeDtypeStruct((8, 128), jnp.float32),
        compiler_params=pltpu.CompilerParams(vmem_limit_bytes=32 * 1024 * 1024, has_side_effects=True),
        name="touch",
    )(*arrays)


def newton(load, state, ratio, strength):
    scale = 0.5 * jnp.exp(ratio * state)
    product = strength * scale
    velocity = load / (product + damping)
    for _ in range(NEWTON):
        scaled = scale * velocity
        magnitude = jnp.abs(scaled)
        root = jnp.sqrt(magnitude * magnitude + 1.0)
        positive = jnp.log(magnitude + root)
        arc = jnp.where(scaled < 0.0, -positive, positive)
        residual = strength * arc + damping * velocity - load
        velocity = velocity - residual / (product / root + damping)
    return velocity


def evolved(state, speed_of):
    return state + time_step * (jnp.exp(-state) - jnp.sqrt(speed_of * speed_of + creep_square))


def scatter_sum(parts):
    lags = len(parts)
    total = parts[0]
    for d in range(1, lags):
        route = [(i, (i + d) % lags) for i in range(lags)]
        total = total + lax.ppermute(parts[d], "lag", route).astype(jnp.float32)
    return total


def settle_friction(shear_load, state, ratio, strength):
    velocity = newton(shear_load, state, ratio, strength)
    return velocity.astype(jnp.bfloat16), evolved(state, velocity)


def tree_to_first(value, lags, least):
    received, stride = [], 1
    while stride < lags:
        route = [(i + stride, i) for i in range(0, lags - stride, 2 * stride) if i + stride >= least]
        arrived = lax.ppermute(value, "lag", route)
        if route[0][1] == 0:
            received.append(arrived)
        stride *= 2
        if stride < lags:
            total = value.astype(jnp.float32) + arrived.astype(jnp.float32)
            value = lax.optimization_barrier(total.astype(jnp.bfloat16))
    return received


def shards(kernel_tiles, shell_index, cone_blocks, history, prestress, log_state, fric_a, fric_b, normal_stress):
    lags = lax.axis_size("lag")
    me = lax.axis_index("lag")
    every, rest = list(range(lags)), list(range(1, lags))
    local = (shell_index, cone_blocks, kernel_tiles)
    field = history[0]
    rows = prestress.shape[2]

    def window_of(own, planes):
        below, above = exchange(own, planes)
        return below, own, above

    def block_load(high, *received):
        load = high
        for part in received:
            load = load + part.astype(jnp.float32)
        return load

    below, own, above = window_of(field, every)
    packed = pack(log_state, fric_a, fric_b, normal_stress)
    packed = [packed] + [lax.ppermute(packed, "lag", [(d, 0)]) for d in rest]
    once = lax.ppermute(field, "lag", [(i, i + 1) for i in every[:-1]])
    touch(kernel_tiles, field)
    traction = scatter_sum(product_by_rows(*local, below, own, above, lags))
    coef_a, coef_b, sigma = (c[0, 0][:, None] for c in (fric_a, fric_b, normal_stress))
    row_pair = (coef_b / coef_a, sigma * coef_a)
    rates, _ = settle_friction(prestress[0, 0] + traction, log_state[0, 0], *row_pair)
    arrived = [lax.ppermute(rates, "lag", [(i, (i + d) % lags) for i in every]) for d in rest]
    first = assemble([rates] + arrived)
    kinds = [jnp.float32, jnp.bfloat16]
    (low,) = block_product(*local, window_of(once, rest), prestress, rest, kinds[1:])
    base_1 = tree_to_first(low, lags, 1)
    twice = lax.ppermute(once, "lag", [(i, i + 1) for i in rest[:-1]])
    window_2 = window_of(twice, rest[1:])
    state, columns = unpack(packed)
    (low,) = block_product(*local, window_2, prestress, rest[1:], kinds[1:])
    base_2 = [lax.ppermute(low, "lag", [(d, 0)]) for d in rest[1:]]

    window = window_of(first, [0, 1])
    high, low = block_product(*local, window, prestress, [0, 1], kinds)
    base_2 = base_2 + [lax.ppermute(low, "lag", [(1, 0)])]

    def on_first(step, *values):
        like = (jax.ShapeDtypeStruct(field.shape, jnp.bfloat16), jax.ShapeDtypeStruct(field.shape, jnp.float32))
        return lax.cond(me == 0, step, lambda *_: tuple(jnp.zeros(x.shape, x.dtype) for x in like), *values)

    def second_step(high, start, first, columns, *received):
        begun = evolved(start, first.astype(jnp.float32))
        return settle_friction(block_load(high, *received), begun, columns[:, 0:1], columns[:, 1:2])

    def third_step(high, start, columns, *received):
        return settle_friction(block_load(high, *received), start, columns[:, 0:1], columns[:, 1:2])

    second, state = on_first(second_step, high, state, first, columns, *base_1)
    window = window_of(second, [0])
    (high,) = block_product(*local, window, prestress, [0], kinds[:1])
    third, state = on_first(third_step, high, state, columns, *base_2)

    source = jnp.where(me == 0, second, twice)
    moved = lax.ppermute(source, "lag", [(0, 1)] + [(i, i + 1) for i in every[2:-1]])
    last = jnp.where(me == 0, third, jnp.where(me == 2, first, moved))
    below, own, above = window_of(last, every)
    mine = state[:rows]
    for d in rest:
        piece = lax.ppermute(state[d * rows : (d + 1) * rows], "lag", [(0, d)])
        mine = jnp.where(me == d, piece, mine)
    traction = scatter_sum(product_by_rows(*local, below, own, above, lags))
    rates, state = settle_friction(prestress[0, 0] + traction, mine, *row_pair)
    return rates[None, None], state[None, None]


def solution(mesh):
    in_specs = (
        P("lag", "elem", None),
        P("lag", "elem", None),
        P("lag"),
        P("lag", "elem", None),
        P("elem", "lag", None, None),
        P("elem", "lag", None, None),
        P("elem", "lag", None),
        P("elem", "lag", None),
        P("elem", "lag", None),
    )
    out_specs = (P("elem", "lag", None, None), P("elem", "lag", None, None))
    return jax.shard_map(shards, mesh=mesh, in_specs=in_specs, out_specs=out_specs, check_vma=False)
```

```python
import functools

import jax
import jax.numpy as jnp
from jax import lax
from jax.experimental import pallas as pl
from jax.experimental.pallas import tpu as pltpu
from jax.sharding import PartitionSpec as P


NEWTON = 3

damping = 0.5
time_step = 0.25
creep_square = 0.01

ANY = pl.BlockSpec(memory_space=pl.ANY)
VMEM = pl.BlockSpec(memory_space=pltpu.VMEM)
PARAMS = pltpu.CompilerParams(vmem_limit_bytes=32 * 1024 * 1024)


def exchange(value, planes):
    count = lax.axis_size("elem")
    up = [(i * count + j, i * count + j + 1) for i in planes for j in range(count - 1)]
    down = [(j, i) for i, j in up]
    axes = ("lag", "elem")
    return lax.ppermute(value, axes, up), lax.ppermute(value, axes, down)


def fetch(picks, live, below, own, above, sources, sems):
    slots = sems.shape[0]
    block = sources.shape[0] // slots
    per = own.shape[0] // block
    alive = live[0]
    for k in range(slots):
        spot = sources.at[pl.ds(k * block, block)]
        pick = picks[0, 0, k]
        start = pl.multiple_of(lax.rem(pick, per) * block, block)
        for which, ref in enumerate((below, own, above)):

            @pl.when((k < alive) & (lax.div(pick, per) == which))
            def _():
                pltpu.make_async_copy(ref.at[pl.ds(start, block)], spot, sems.at[k]).start()

    for k in range(slots):
        spot = sources.at[pl.ds(k * block, block)]

        @pl.when(k >= alive)
        def _():
            spot[...] = jnp.zeros(spot.shape, spot.dtype)

        @pl.when(k < alive)
        def _():
            pltpu.make_async_copy(own.at[pl.ds(0, block)], spot, sems.at[k]).wait()


def rows_kernel(lags, rows, picks, live, tile, below, own, above, *refs):
    outs, sources, sems = refs[:lags], refs[lags], refs[lags + 1]
    me = lax.axis_index("lag")
    fetch(picks, live, below, own, above, sources, sems)
    for d in range(lags):
        first = pl.multiple_of(lax.rem(me + d, lags) * rows, rows)
        part = jnp.dot(tile[0, pl.ds(first, rows), :], sources[...], preferred_element_type=jnp.float32)
        outs[d][...] = part.astype(outs[d].dtype)


def product_by_rows(picks, live, tile, below, own, above, lags):
    rows, cols = own.shape[0] // lags, own.shape[1]
    kinds = [jnp.float32] + [jnp.bfloat16] * (lags - 1)
    return pl.pallas_call(
        functools.partial(rows_kernel, lags, rows),
        grid_spec=pltpu.PrefetchScalarGridSpec(
            num_scalar_prefetch=2,
            grid=(1,),
            in_specs=[VMEM] + [ANY] * 3,
            out_specs=[VMEM] * lags,
            scratch_shapes=[pltpu.VMEM((tile.shape[2], cols), own.dtype), pltpu.SemaphoreType.DMA((picks.shape[2],))],
        ),
        out_shape=[jax.ShapeDtypeStruct((rows, cols), kind) for kind in kinds],
        compiler_params=PARAMS,
        cost_estimate=pl.CostEstimate(
            flops=2 * tile.size * cols, bytes_accessed=2 * (tile.size + 4 * own.size), transcendentals=0
        ),
        name="product_by_rows",
    )(picks, live, tile, below, own, above)


def block_kernel(chunks, planes, high_too, picks, live, tile, below, own, above, stress, *refs):
    outs, sources, sems = refs[:-2], refs[-2], refs[-1]
    me = lax.axis_index("lag")
    rows, height = own.shape[0] // chunks, stress.shape[2]
    mine = pl.ds(pl.multiple_of(me * height, height), height)

    def write(out):
        for d in range(chunks):
            spot = pl.ds(d * rows, rows)
            part = jnp.dot(tile[0, spot, :], sources[...], preferred_element_type=jnp.float32)
            out[spot, :] = part.astype(out.dtype)
        part = jnp.dot(tile[0, mine, :], sources[...], preferred_element_type=jnp.float32)
        out[mine, :] = (part + stress[0, 0]).astype(out.dtype)

    @pl.when((me >= planes[0]) & (me <= planes[-1]))
    def _():
        fetch(picks, live, below, own, above, sources, sems)
        if high_too:

            @pl.when(me == 0)
            def _():
                write(outs[0])

            @pl.when(me > 0)
            def _():
                write(outs[1])

        else:
            write(outs[0])


def block_product(picks, live, tile, window, stress, planes, kinds):
    below, own, above = window
    chunks = max(1, tile.shape[1] // 256)
    return pl.pallas_call(
        functools.partial(block_kernel, chunks, (planes[0], planes[-1]), len(kinds) > 1),
        grid_spec=pltpu.PrefetchScalarGridSpec(
            num_scalar_prefetch=2,
            grid=(1,),
            in_specs=[VMEM] + [ANY] * 3 + [VMEM],
            out_specs=[VMEM] * len(kinds),
            scratch_shapes=[
                pltpu.VMEM((tile.shape[2], own.shape[1]), own.dtype),
                pltpu.SemaphoreType.DMA((picks.shape[2],)),
            ],
        ),
        out_shape=[jax.ShapeDtypeStruct(own.shape, kind) for kind in kinds],
        compiler_params=PARAMS,
        cost_estimate=pl.CostEstimate(
            flops=2 * tile.size * own.shape[1], bytes_accessed=2 * (tile.size + 4 * own.size), transcendentals=0
        ),
        name="block_product",
    )(picks, live, tile, below, own, above, stress)


def pack_kernel(state, coef_a, coef_b, sigma, out):
    rows = state.shape[2]
    out[pl.ds(0, rows), :] = state[0, 0]
    out[pl.ds(rows, 8), :] = jnp.zeros((8, out.shape[1]), out.dtype)
    out[pl.ds(rows, 1), pl.ds(0, rows)] = coef_b[0] / coef_a[0]
    out[pl.ds(rows + 1, 1), pl.ds(0, rows)] = sigma[0] * coef_a[0]


def pack(state, coef_a, coef_b, sigma):
    return pl.pallas_call(
        pack_kernel,
        in_specs=[VMEM] * 4,
        out_specs=VMEM,
        out_shape=jax.ShapeDtypeStruct((state.shape[2] + 8, state.shape[3]), jnp.float32),
        compiler_params=PARAMS,
        name="pack",
    )(state, coef_a, coef_b, sigma)


def unpack_kernel(lags, *refs):
    packed, state, coefs = refs[:lags], refs[lags], refs[lags + 1]
    rows = state.shape[0] // lags

    @pl.when(lax.axis_index("lag") == 0)
    def _():
        for d, ref in enumerate(packed):
            spot = pl.ds(d * rows, rows)
            state[spot, :] = ref[pl.ds(0, rows), :]
            coefs[d] = ref[pl.ds(rows, 8), :]


def unpack(packed):
    lags, (height, cols) = len(packed), packed[0].shape
    rows = (height - 8) * lags
    state, coefs = pl.pallas_call(
        functools.partial(unpack_kernel, lags),
        in_specs=[VMEM] * lags,
        out_specs=[VMEM] * 2,
        out_shape=[jax.ShapeDtypeStruct((rows, cols), jnp.float32), jax.ShapeDtypeStruct((lags, 8, cols), jnp.float32)],
        compiler_params=PARAMS,
        name="unpack",
    )(*packed)
    return state, *(coefs[:, k, : rows // lags].reshape(rows) for k in range(2))


def assemble_kernel(*refs):
    parts, out = refs[:-1], refs[-1]
    me, lags = lax.axis_index("lag"), len(parts)
    rows = parts[0].shape[0]
    for d, part in enumerate(parts):
        spot = pl.multiple_of(lax.rem(me + lags - d, lags) * rows, rows)
        out[pl.ds(spot, rows), :] = part[...]


def assemble(parts):
    rows, cols = parts[0].shape
    return pl.pallas_call(
        assemble_kernel,
        in_specs=[VMEM] * len(parts),
        out_specs=VMEM,
        out_shape=jax.ShapeDtypeStruct((rows * len(parts), cols), parts[0].dtype),
        compiler_params=PARAMS,
        name="assemble",
    )(*parts)


def touch(*arrays):
    pl.pallas_call(
        lambda *refs: refs[-1].__setitem__(Ellipsis, jnp.zeros(refs[-1].shape, refs[-1].dtype)),
        in_specs=[ANY] * len(arrays),
        out_specs=VMEM,
        out_shape=jax.ShapeDtypeStruct((8, 128), jnp.float32),
        compiler_params=pltpu.CompilerParams(vmem_limit_bytes=32 * 1024 * 1024, has_side_effects=True),
        name="touch",
    )(*arrays)


def newton(load, state, ratio, strength):
    scale = 0.5 * jnp.exp(ratio * state)
    product = strength * scale
    velocity = load / (product + damping)
    for _ in range(NEWTON):
        scaled = scale * velocity
        magnitude = jnp.abs(scaled)
        root = jnp.sqrt(magnitude * magnitude + 1.0)
        positive = jnp.log(magnitude + root)
        arc = jnp.where(scaled < 0.0, -positive, positive)
        residual = strength * arc + damping * velocity - load
        velocity = velocity - residual / (product / root + damping)
    return velocity


def evolved(state, speed_of):
    return state + time_step * (jnp.exp(-state) - jnp.sqrt(speed_of * speed_of + creep_square))


def scatter_sum(parts):
    lags = len(parts)
    total = parts[0]
    for d in range(1, lags):
        route = [(i, (i + d) % lags) for i in range(lags)]
        total = total + lax.ppermute(parts[d], "lag", route).astype(jnp.float32)
    return total


def settle_friction(shear_load, state, ratio, strength):
    velocity = newton(shear_load, state, ratio, strength)
    return velocity.astype(jnp.bfloat16), evolved(state, velocity)


def tree_to_first(value, lags, least):
    received, stride = [], 1
    while stride < lags:
        route = [(i + stride, i) for i in range(0, lags - stride, 2 * stride) if i + stride >= least]
        arrived = lax.ppermute(value, "lag", route)
        if route[0][1] == 0:
            received.append(arrived)
        stride *= 2
        if stride < lags:
            total = value.astype(jnp.float32) + arrived.astype(jnp.float32)
            value = lax.optimization_barrier(total.astype(jnp.bfloat16))
    return received


def shards(kernel_tiles, shell_index, cone_blocks, history, prestress, log_state, fric_a, fric_b, normal_stress):
    lags = lax.axis_size("lag")
    me = lax.axis_index("lag")
    every, rest = list(range(lags)), list(range(1, lags))
    local = (shell_index, cone_blocks, kernel_tiles)
    field = history[0]
    rows = prestress.shape[2]

    def window_of(own, planes):
        below, above = exchange(own, planes)
        return below, own, above

    def block_load(high, *received):
        load = high
        for part in received:
            load = load + part.astype(jnp.float32)
        return load

    below, own, above = window_of(field, every)
    packed = pack(log_state, fric_a, fric_b, normal_stress)
    packed = [packed] + [lax.ppermute(packed, "lag", [(d, 0)]) for d in rest]
    once = lax.ppermute(field, "lag", [(i, i + 1) for i in every[:-1]])
    touch(kernel_tiles, field)
    traction = scatter_sum(product_by_rows(*local, below, own, above, lags))
    coef_a, coef_b, sigma = (c[0, 0][:, None] for c in (fric_a, fric_b, normal_stress))
    row_pair = (coef_b / coef_a, sigma * coef_a)
    rates, _ = settle_friction(prestress[0, 0] + traction, log_state[0, 0], *row_pair)
    arrived = [lax.ppermute(rates, "lag", [(i, (i + d) % lags) for i in every]) for d in rest]
    first = assemble([rates] + arrived)
    kinds = [jnp.float32, jnp.bfloat16]
    (low,) = block_product(*local, window_of(once, rest), prestress, rest, kinds[1:])
    base_1 = tree_to_first(low, lags, 1)
    twice = lax.ppermute(once, "lag", [(i, i + 1) for i in rest[:-1]])
    window_2 = window_of(twice, rest[1:])
    state, *coefs = unpack(packed)
    (low,) = block_product(*local, window_2, prestress, rest[1:], kinds[1:])
    base_2 = [lax.ppermute(low, "lag", [(d, 0)]) for d in rest[1:]]

    window = window_of(first, [0, 1])
    high, low = block_product(*local, window, prestress, [0, 1], kinds)
    base_2 = base_2 + [lax.ppermute(low, "lag", [(1, 0)])]

    def nothing(high, start, first, *values):
        return jnp.zeros(first.shape, first.dtype), jnp.zeros(start.shape, start.dtype)

    def second_step(high, start, first, ratio, strength, *received):
        begun = evolved(start, first.astype(jnp.float32))
        return settle_friction(block_load(high, *received), begun, ratio[:, None], strength[:, None])

    def third_step(high, start, ratio, strength, first, moved, *received):
        return settle_friction(block_load(high, *received), start, ratio[:, None], strength[:, None])

    def last_field(high, start, ratio, strength, first, moved, *received):
        return jnp.where(me == 2, first, moved), jnp.zeros(start.shape, start.dtype)

    second, state = lax.cond(me == 0, second_step, nothing, high, state, first, *coefs, *base_1)
    window = window_of(second, [0])
    (high,) = block_product(*local, window, prestress, [0], kinds[:1])
    source = jnp.where(me == 0, second, twice)
    moved = lax.ppermute(source, "lag", [(0, 1)] + [(i, i + 1) for i in every[2:-1]])
    values = (high, state, *coefs, first, moved, *base_2)
    last, state = lax.cond(me == 0, third_step, last_field, *values)

    below, own, above = window_of(last, every)
    mine = state[:rows]
    for d in rest:
        piece = lax.ppermute(state[d * rows : (d + 1) * rows], "lag", [(0, d)])
        mine = jnp.where(me == d, piece, mine)
    traction = scatter_sum(product_by_rows(*local, below, own, above, lags))
    rates, state = settle_friction(prestress[0, 0] + traction, mine, *row_pair)
    return rates[None, None], state[None, None]


def solution(mesh):
    in_specs = (
        P("lag", "elem", None),
        P("lag", "elem", None),
        P("lag"),
        P("lag", "elem", None),
        P("elem", "lag", None, None),
        P("elem", "lag", None, None),
        P("elem", "lag", None),
        P("elem", "lag", None),
        P("elem", "lag", None),
    )
    out_specs = (P("elem", "lag", None, None), P("elem", "lag", None, None))
    return jax.shard_map(shards, mesh=mesh, in_specs=in_specs, out_specs=out_specs, check_vma=False)
```

```python
import functools

import jax
import jax.numpy as jnp
from jax import lax
from jax.experimental import pallas as pl
from jax.experimental.pallas import tpu as pltpu
from jax.sharding import PartitionSpec as P


NEWTON = 3

damping = 0.5
time_step = 0.25
creep_square = 0.01

ANY = pl.BlockSpec(memory_space=pl.ANY)
VMEM = pl.BlockSpec(memory_space=pltpu.VMEM)
PARAMS = pltpu.CompilerParams(vmem_limit_bytes=32 * 1024 * 1024)


def exchange(value, planes):
    count = lax.axis_size("elem")
    up = [(i * count + j, i * count + j + 1) for i in planes for j in range(count - 1)]
    down = [(j, i) for i, j in up]
    axes = ("lag", "elem")
    return lax.ppermute(value, axes, up), lax.ppermute(value, axes, down)


def fetch(picks, live, below, own, above, sources, sems):
    slots = sems.shape[0]
    block = sources.shape[0] // slots
    per = own.shape[0] // block
    alive = live[0]
    for k in range(slots):
        spot = sources.at[pl.ds(k * block, block)]
        pick = picks[0, 0, k]
        start = pl.multiple_of(lax.rem(pick, per) * block, block)
        for which, ref in enumerate((below, own, above)):

            @pl.when((k < alive) & (lax.div(pick, per) == which))
            def _():
                pltpu.make_async_copy(ref.at[pl.ds(start, block)], spot, sems.at[k]).start()

    for k in range(slots):
        spot = sources.at[pl.ds(k * block, block)]

        @pl.when(k >= alive)
        def _():
            spot[...] = jnp.zeros(spot.shape, spot.dtype)

        @pl.when(k < alive)
        def _():
            pltpu.make_async_copy(own.at[pl.ds(0, block)], spot, sems.at[k]).wait()


def rows_kernel(lags, rows, picks, live, tile, below, own, above, *refs):
    outs, sources, sems = refs[:lags], refs[lags], refs[lags + 1]
    me = lax.axis_index("lag")
    fetch(picks, live, below, own, above, sources, sems)
    for d in range(lags):
        first = pl.multiple_of(lax.rem(me + d, lags) * rows, rows)
        part = jnp.dot(tile[0, pl.ds(first, rows), :], sources[...], preferred_element_type=jnp.float32)
        outs[d][...] = part.astype(outs[d].dtype)


def product_by_rows(picks, live, tile, below, own, above, lags):
    rows, cols = own.shape[0] // lags, own.shape[1]
    kinds = [jnp.float32] + [jnp.bfloat16] * (lags - 1)
    return pl.pallas_call(
        functools.partial(rows_kernel, lags, rows),
        grid_spec=pltpu.PrefetchScalarGridSpec(
            num_scalar_prefetch=2,
            grid=(1,),
            in_specs=[VMEM] + [ANY] * 3,
            out_specs=[VMEM] * lags,
            scratch_shapes=[pltpu.VMEM((tile.shape[2], cols), own.dtype), pltpu.SemaphoreType.DMA((picks.shape[2],))],
        ),
        out_shape=[jax.ShapeDtypeStruct((rows, cols), kind) for kind in kinds],
        compiler_params=PARAMS,
        cost_estimate=pl.CostEstimate(
            flops=2 * tile.size * cols, bytes_accessed=2 * (tile.size + 4 * own.size), transcendentals=0
        ),
        name="product_by_rows",
    )(picks, live, tile, below, own, above)


def block_kernel(chunks, planes, high_too, picks, live, tile, below, own, above, stress, *refs):
    outs, sources, sems = refs[:-2], refs[-2], refs[-1]
    me = lax.axis_index("lag")
    rows, height = own.shape[0] // chunks, stress.shape[2]
    mine = pl.ds(pl.multiple_of(me * height, height), height)

    def write(out):
        for d in range(chunks):
            spot = pl.ds(d * rows, rows)
            part = jnp.dot(tile[0, spot, :], sources[...], preferred_element_type=jnp.float32)
            out[spot, :] = part.astype(out.dtype)
        part = jnp.dot(tile[0, mine, :], sources[...], preferred_element_type=jnp.float32)
        out[mine, :] = (part + stress[0, 0]).astype(out.dtype)

    @pl.when((me >= planes[0]) & (me <= planes[-1]))
    def _():
        fetch(picks, live, below, own, above, sources, sems)
        if high_too:

            @pl.when(me == 0)
            def _():
                write(outs[0])

            @pl.when(me > 0)
            def _():
                write(outs[1])

        else:
            write(outs[0])


def block_product(picks, live, tile, window, stress, planes, kinds):
    below, own, above = window
    chunks = max(1, tile.shape[1] // 256)
    return pl.pallas_call(
        functools.partial(block_kernel, chunks, (planes[0], planes[-1]), len(kinds) > 1),
        grid_spec=pltpu.PrefetchScalarGridSpec(
            num_scalar_prefetch=2,
            grid=(1,),
            in_specs=[VMEM] + [ANY] * 3 + [VMEM],
            out_specs=[VMEM] * len(kinds),
            scratch_shapes=[
                pltpu.VMEM((tile.shape[2], own.shape[1]), own.dtype),
                pltpu.SemaphoreType.DMA((picks.shape[2],)),
            ],
        ),
        out_shape=[jax.ShapeDtypeStruct(own.shape, kind) for kind in kinds],
        compiler_params=PARAMS,
        cost_estimate=pl.CostEstimate(
            flops=2 * tile.size * own.shape[1], bytes_accessed=2 * (tile.size + 4 * own.size), transcendentals=0
        ),
        name="block_product",
    )(picks, live, tile, below, own, above, stress)


def pack_kernel(state, coef_a, coef_b, sigma, out):
    rows = state.shape[2]
    out[pl.ds(0, rows), :] = state[0, 0]
    out[pl.ds(rows, 8), :] = jnp.zeros((8, out.shape[1]), out.dtype)
    out[pl.ds(rows, 1), pl.ds(0, rows)] = coef_b[0] / coef_a[0]
    out[pl.ds(rows + 1, 1), pl.ds(0, rows)] = sigma[0] * coef_a[0]


def pack(state, coef_a, coef_b, sigma):
    return pl.pallas_call(
        pack_kernel,
        in_specs=[VMEM] * 4,
        out_specs=VMEM,
        out_shape=jax.ShapeDtypeStruct((state.shape[2] + 8, state.shape[3]), jnp.float32),
        compiler_params=PARAMS,
        name="pack",
    )(state, coef_a, coef_b, sigma)


def unpack_kernel(lags, *refs):
    packed, state, coefs = refs[:lags], refs[lags], refs[lags + 1]
    rows = state.shape[0] // lags

    @pl.when(lax.axis_index("lag") == 0)
    def _():
        for d, ref in enumerate(packed):
            spot = pl.ds(d * rows, rows)
            state[spot, :] = ref[pl.ds(0, rows), :]
            coefs[d] = ref[pl.ds(rows, 8), :]


def unpack(packed):
    lags, (height, cols) = len(packed), packed[0].shape
    rows = (height - 8) * lags
    state, coefs = pl.pallas_call(
        functools.partial(unpack_kernel, lags),
        in_specs=[VMEM] * lags,
        out_specs=[VMEM] * 2,
        out_shape=[jax.ShapeDtypeStruct((rows, cols), jnp.float32), jax.ShapeDtypeStruct((lags, 8, cols), jnp.float32)],
        compiler_params=PARAMS,
        name="unpack",
    )(*packed)
    return state, *(coefs[:, k, : rows // lags].reshape(rows) for k in range(2))


def assemble_kernel(*refs):
    parts, out = refs[:-1], refs[-1]
    me, lags = lax.axis_index("lag"), len(parts)
    rows = parts[0].shape[0]
    for d, part in enumerate(parts):
        spot = pl.multiple_of(lax.rem(me + lags - d, lags) * rows, rows)
        out[pl.ds(spot, rows), :] = part[...]


def assemble(parts):
    rows, cols = parts[0].shape
    return pl.pallas_call(
        assemble_kernel,
        in_specs=[VMEM] * len(parts),
        out_specs=VMEM,
        out_shape=jax.ShapeDtypeStruct((rows * len(parts), cols), parts[0].dtype),
        compiler_params=PARAMS,
        name="assemble",
    )(*parts)


def touch(*arrays):
    pl.pallas_call(
        lambda *refs: refs[-1].__setitem__(Ellipsis, jnp.zeros(refs[-1].shape, refs[-1].dtype)),
        in_specs=[ANY] * len(arrays),
        out_specs=VMEM,
        out_shape=jax.ShapeDtypeStruct((8, 128), jnp.float32),
        compiler_params=pltpu.CompilerParams(vmem_limit_bytes=32 * 1024 * 1024, has_side_effects=True),
        name="touch",
    )(*arrays)


def newton(load, state, ratio, strength):
    scale = 0.5 * jnp.exp(ratio * state)
    product = strength * scale
    velocity = load / (product + damping)
    for _ in range(NEWTON):
        scaled = scale * velocity
        magnitude = jnp.abs(scaled)
        root = jnp.sqrt(magnitude * magnitude + 1.0)
        positive = jnp.log(magnitude + root)
        arc = jnp.where(scaled < 0.0, -positive, positive)
        residual = strength * arc + damping * velocity - load
        velocity = velocity - residual / (product / root + damping)
    return velocity


def evolved(state, speed_of):
    return state + time_step * (jnp.exp(-state) - jnp.sqrt(speed_of * speed_of + creep_square))


def scatter_sum(parts):
    lags = len(parts)
    total = parts[0]
    for d in range(1, lags):
        route = [(i, (i + d) % lags) for i in range(lags)]
        total = total + lax.ppermute(parts[d], "lag", route).astype(jnp.float32)
    return total


def settle_friction(shear_load, state, ratio, strength):
    velocity = newton(shear_load, state, ratio, strength)
    return velocity.astype(jnp.bfloat16), evolved(state, velocity)


def tree_to_first(value, lags, least):
    received, stride = [], 1
    while stride < lags:
        route = [(i + stride, i) for i in range(0, lags - stride, 2 * stride) if i + stride >= least]
        arrived = lax.ppermute(value, "lag", route)
        if route[0][1] == 0:
            received.append(arrived)
        stride *= 2
        if stride < lags:
            total = value.astype(jnp.float32) + arrived.astype(jnp.float32)
            value = lax.optimization_barrier(total.astype(jnp.bfloat16))
    return received


def shards(kernel_tiles, shell_index, cone_blocks, history, prestress, log_state, fric_a, fric_b, normal_stress):
    lags = lax.axis_size("lag")
    me = lax.axis_index("lag")
    every, rest = list(range(lags)), list(range(1, lags))
    local = (shell_index, cone_blocks, kernel_tiles)
    field = history[0]
    rows = prestress.shape[2]

    def window_of(own, planes):
        below, above = exchange(own, planes)
        return below, own, above

    def block_load(high, *received):
        load = high
        for part in received:
            load = load + part.astype(jnp.float32)
        return load

    below, own, above = window_of(field, every)
    packed = pack(log_state, fric_a, fric_b, normal_stress)
    packed = [packed] + [lax.ppermute(packed, "lag", [(d, 0)]) for d in rest]
    once = lax.ppermute(field, "lag", [(i, i + 1) for i in every[:-1]])
    touch(kernel_tiles, field)
    traction = scatter_sum(product_by_rows(*local, below, own, above, lags))
    coef_a, coef_b, sigma = (c[0, 0][:, None] for c in (fric_a, fric_b, normal_stress))
    row_pair = (coef_b / coef_a, sigma * coef_a)
    rates, row_state = settle_friction(prestress[0, 0] + traction, log_state[0, 0], *row_pair)
    arrived = [lax.ppermute(rates, "lag", [(i, (i + d) % lags) for i in every]) for d in rest]
    first = assemble([rates] + arrived)
    kinds = [jnp.float32, jnp.bfloat16]
    (low,) = block_product(*local, window_of(once, rest), prestress, rest, kinds[1:])
    base_1 = tree_to_first(low, lags, 1)
    twice = lax.ppermute(once, "lag", [(i, i + 1) for i in rest[:-1]])
    window_2 = window_of(twice, rest[1:])
    state, *coefs = unpack(packed)
    (low,) = block_product(*local, window_2, prestress, rest[1:], kinds[1:])
    base_2 = tree_to_first(low, lags, 2)

    window = window_of(first, [0, 1])
    high, low = block_product(*local, window, prestress, [0, 1], kinds)
    base_2 = base_2 + [lax.ppermute(low, "lag", [(1, 0)])]

    def nothing(high, start, first, *values):
        return jnp.zeros(first.shape, first.dtype), jnp.zeros(start.shape, start.dtype)

    def second_step(high, start, first, ratio, strength, *received):
        return settle_friction(block_load(high, *received), start, ratio[:, None], strength[:, None])

    def third_step(high, start, ratio, strength, first, moved, *received):
        return settle_friction(block_load(high, *received), start, ratio[:, None], strength[:, None])

    def last_field(high, start, ratio, strength, first, moved, *received):
        return jnp.where(me == 2, first, moved), jnp.zeros(start.shape, start.dtype)

    begun = lax.optimization_barrier(evolved(state, first.astype(jnp.float32)))
    second, state = lax.cond(me == 0, second_step, nothing, high, begun, first, *coefs, *base_1)
    window = window_of(second, [0])
    (high,) = block_product(*local, window, prestress, [0], kinds[:1])
    source = jnp.where(me == 0, second, twice)
    moved = lax.ppermute(source, "lag", [(0, 1)] + [(i, i + 1) for i in every[2:-1]])
    values = (high, state, *coefs, first, moved, *base_2)
    last, state = lax.cond(me == 0, third_step, last_field, *values)

    below, own, above = window_of(last, every)
    change = (state - begun).astype(jnp.bfloat16)
    mine = change[:rows]
    for d in rest:
        piece = lax.ppermute(change[d * rows : (d + 1) * rows], "lag", [(0, d)])
        mine = jnp.where(me == d, piece, mine)
    mine = row_state + mine.astype(jnp.float32)
    traction = scatter_sum(product_by_rows(*local, below, own, above, lags))
    rates, state = settle_friction(prestress[0, 0] + traction, mine, *row_pair)
    return rates[None, None], state[None, None]


def solution(mesh):
    in_specs = (
        P("lag", "elem", None),
        P("lag", "elem", None),
        P("lag"),
        P("lag", "elem", None),
        P("elem", "lag", None, None),
        P("elem", "lag", None, None),
        P("elem", "lag", None),
        P("elem", "lag", None),
        P("elem", "lag", None),
    )
    out_specs = (P("elem", "lag", None, None), P("elem", "lag", None, None))
    return jax.shard_map(shards, mesh=mesh, in_specs=in_specs, out_specs=out_specs, check_vma=False)
```
